256 devices in a mesh: row: 16 (over z, core), col: 16 (over x, y).
Axes of the slice: x: 4, y: 4, z: 8, core: 2. Of those that a mesh axis runs over, the one named last changes fastest.
Arguments:
- child_samples: bfloat16 [2, 2, 256, 262144], P(None, None, 'col', 'row'), may hold values from -6 to 6
- child_map: int32 [2, 2048], P(None, 'row'), may hold values from 0 to 127, as said below
- forward_probe: bfloat16 [256, 262144], P(None, ('row', 'col')), may hold values from -6 to 6
- adjoint_probe: bfloat16 [256, 262144], P(None, ('row', 'col')), may hold values from -6 to 6
- stored_sparse_blocks: bfloat16 [2048, 18, 128, 128], P(('row', 'col')), may hold values from -0.125 to 0.125
- block_pattern: int32 [16, 128, 18], P(None, 'col'), may hold values from 0 to 7
Outputs:
- row_basis: bfloat16 [256, 262144], P(None, ('row', 'col'))
- column_basis: bfloat16 [256, 262144], P(None, ('row', 'col'))
- transfers: float32 [2, 2, 65536, 256], P(None, None, ('row', 'col'))
The draws below stay inside these ranges and needn't reach their ends.
Inputs may be any that keep to these rules, and one draw needn't show every extreme that they name: Within each aligned group of 16 * 8 front blocks (one row group), each row of child_map is a permutation of 0 to 16 * 8 - 1.
All inputs are finite; a program needn't handle non-finite values.
Results may differ from the reference program's by a relative error of at most 0.0055.
Values may be sent and summed in bfloat16 or wider, within the bound.
A program may use at most 128 MiB of HBM per device.

```python
import math
from functools import partial
import jax
import jax.numpy as jnp
from jax import lax

S = 256
BLK = 128
SLOTS = 6
R_DEV = 1024
BLK_DEV = 8
N = 262144
N_ROW = 16
N_COL = 16
DEVICES = 256


def draw_child_map(key, part):
    group_blocks = N_COL * BLK_DEV
    keys = jax.random.split(jax.random.fold_in(key, 17), 2 * N_ROW)
    perms = jax.vmap(lambda single: jax.random.permutation(single, group_blocks))(keys)
    return perms.reshape(2, N_ROW * group_blocks).astype(jnp.int32)


def plant(array, key, low, largest):
    longest = array.shape.index(max(array.shape))
    spots = []
    for shift in (0, 1):
        where = [jax.random.randint(jax.random.fold_in(key, axis), (), 0, length) for axis, length in enumerate(array.shape)]
        where[longest] = (where[longest] + shift) % array.shape[longest]
        spots.append(tuple(where))
    return array.at[spots[0]].set(low).at[spots[1]].set(largest)


def block_scale(key, extent, pieces, low, largest):
    gain = 1.0
    for dim, shards_of in pieces:
        heights = jax.random.uniform(jax.random.fold_in(jax.random.fold_in(key, 6), dim), (shards_of,), jnp.float32, low / len(pieces), largest / len(pieces))
        gain = gain * jnp.repeat(jnp.exp(heights), extent[dim] // shards_of).reshape((-1,) + (1,) * (len(extent) - 1 - dim))
    return gain


def centred(stream_key, extent, width, most, shards=(), kind=jnp.bfloat16):
    result = width * jax.random.normal(stream_key, extent, jnp.float32)
    if shards:
        result = result * block_scale(stream_key, extent, shards, -0.22, 0.18)
    return jnp.clip(result, -most, most).astype(kind)


def setup_inputs(seed: int = 0) -> dict:
    streams_of = jax.random.split(jax.random.key(seed), 7)
    return {
        "child_samples": centred(streams_of[0], (2, 2, S, N), 1.0, 6.0, ((2, 16), (3, 16))),
        "child_map": draw_child_map(jax.random.fold_in(streams_of[6], 71), 0),
        "forward_probe": centred(streams_of[2], (S, N), 1.0, 6.0, ((1, 256),)),
        "adjoint_probe": centred(streams_of[3], (S, N), 1.0, 6.0, ((1, 256),)),
        "stored_sparse_blocks": centred(streams_of[4], (N // BLK, 3 * SLOTS, BLK, BLK), (3 * SLOTS * BLK) ** -0.5, 0.125, ((0, 256),)),
        "block_pattern": plant(jax.random.randint(streams_of[5], (N_ROW, N_COL * BLK_DEV, 3 * SLOTS), 0, BLK_DEV), jax.random.fold_in(streams_of[5], 1), 0, BLK_DEV - 1).astype(jnp.int32),
    }


def reference(child_samples, child_map, forward_probe, adjoint_probe, stored_sparse_blocks, block_pattern):
    group_blocks = N_COL * BLK_DEV
    total_blocks = N // BLK
    slot_count = 3 * SLOTS
    blocked = child_samples.reshape(2, 2, S, N_ROW, group_blocks, BLK)
    maps = child_map.reshape(2, N_ROW, group_blocks)

    def pick(source, indices):
        return jnp.take(source, indices, axis=2)
    picked = [jax.vmap(pick, in_axes=(2, 0), out_axes=2)(blocked[child], maps[child]).astype(jnp.float32) for child in range(2)]
    extended = (picked[0] + picked[1]).astype(jnp.bfloat16).reshape(2, S, N)
    patterns = block_pattern.reshape(DEVICES, BLK_DEV, slot_count)
    regions = jnp.arange(slot_count, dtype=jnp.int32) // SLOTS
    probe_blocks = forward_probe.reshape(S, total_blocks, BLK).astype(jnp.float32)
    adjoint_blocks = adjoint_probe.reshape(S, total_blocks, BLK).astype(jnp.float32)
    matrices = stored_sparse_blocks.reshape(DEVICES, BLK_DEV, slot_count, BLK, BLK)

    def columns(device):
        group_row = device // N_COL
        neighbour = group_row + regions - 1
        valid_entries = ((neighbour >= 0) & (neighbour < N_ROW)).astype(jnp.float32)
        target = device * BLK_DEV + (regions - 1) * group_blocks + patterns[device]
        target = jnp.clip(target, 0, total_blocks - 1).astype(jnp.int32)
        return (target, valid_entries)

    def forward_part(device):
        target, valid_entries = columns(device)
        collected_samples = jnp.take(probe_blocks, target, axis=1) * valid_entries[None, None, :, None]
        resident_part = matrices[device].astype(jnp.float32)
        return jnp.einsum('wjht,jhot->wjo', collected_samples, resident_part)
    forward_sparse = lax.map(forward_part, jnp.arange(DEVICES, dtype=jnp.int32))
    forward_sparse = jnp.transpose(forward_sparse, (1, 0, 2, 3)).reshape(S, N)

    def adjoint_step(carry, device):
        target, valid_entries = columns(device)
        sample_rows = lax.dynamic_slice_in_dim(adjoint_blocks, (device * BLK_DEV).astype(jnp.int32), BLK_DEV, 1)
        resident_part = matrices[device].astype(jnp.float32)
        sketch_products = jnp.einsum('mda,duai->dumi', sample_rows, resident_part) * valid_entries[None, :, None, None]
        carry = carry.at[target.reshape(-1)].add(sketch_products.reshape(BLK_DEV * slot_count, S, BLK))
        return (carry, None)
    adjoint_sparse, _ = lax.scan(adjoint_step, jnp.zeros((total_blocks, S, BLK), jnp.float32), jnp.arange(DEVICES, dtype=jnp.int32))
    adjoint_sparse = jnp.transpose(adjoint_sparse, (1, 0, 2)).reshape(S, N)
    samples = jnp.stack([extended[0].astype(jnp.float32) + forward_sparse, extended[1].astype(jnp.float32) + adjoint_sparse])
    leaves = samples.reshape(2, S, DEVICES, R_DEV).transpose(0, 2, 1, 3)
    grams = jnp.einsum('kdsr,kdtr->kdst', leaves, leaves, precision=lax.Precision.HIGHEST)
    level_one = grams.reshape(2, DEVICES // 2, 2, S, S).sum(axis=2)
    level_two = level_one.reshape(2, DEVICES // 4, 2, S, S).sum(axis=2)
    factor_leaf = jnp.linalg.cholesky(grams)
    factor_one = jnp.repeat(jnp.linalg.cholesky(level_one), 2, axis=1)
    factor_two = jnp.repeat(jnp.linalg.cholesky(level_two), 4, axis=1)
    solver = jax.vmap(jax.vmap(partial(jax.scipy.linalg.solve_triangular, lower=True)))
    bases = solver(factor_leaf, leaves) * math.sqrt(R_DEV)
    first = jnp.swapaxes(solver(factor_one, factor_leaf), -1, -2)
    second = jnp.swapaxes(solver(factor_two, factor_one), -1, -2)
    transfers = jnp.stack([first, second], axis=1).reshape(2, 2, DEVICES * S, S)
    bases = bases.transpose(0, 2, 1, 3).reshape(2, S, N).astype(jnp.bfloat16)
    return (bases[0], bases[1], transfers)
```

```python
import math

import jax
import jax.numpy as jnp
from jax import lax
from jax.experimental import pallas as pl
from jax.experimental.pallas import tpu as pltpu
from jax.sharding import PartitionSpec as P

S = 256
BLK = 128
SLOTS = 6
PANEL = 32
PITCH = S + 8
F32 = jnp.float32
BF16 = jnp.bfloat16
HIGHEST = lax.Precision.HIGHEST
VMEM_LIMIT = 56 << 20


def params():
    return pltpu.CompilerParams(vmem_limit_bytes=VMEM_LIMIT)


def split3(x):
    high = x.astype(BF16)
    rest = x - high.astype(F32)
    mid = rest.astype(BF16)
    low = (rest - mid.astype(F32)).astype(BF16)
    return high, mid, low


def dot3(a, b, dims):
    ah, am, _ = split3(a)
    bh, bm, _ = split3(b)
    dn = (dims, ((), ()))
    out = lax.dot_general(ah, bh, dn, preferred_element_type=F32)
    out += lax.dot_general(ah, bm, dn, preferred_element_type=F32)
    out += lax.dot_general(am, bh, dn, preferred_element_type=F32)
    return out


def extend_kernel(map_ref, child_ref, out_ref):
    leaves = out_ref.shape[0]
    blocks = out_ref.shape[3] // BLK

    def leaf(d, carry):
        for b in range(blocks):
            first = pl.multiple_of(map_ref[0, d * blocks + b] * BLK, BLK)
            second = pl.multiple_of(map_ref[1, d * blocks + b] * BLK, BLK)
            for k in range(2):
                x = child_ref[0, k, :, pl.ds(first, BLK)].astype(F32)
                y = child_ref[1, k, :, pl.ds(second, BLK)].astype(F32)
                out_ref[d, k, :, b * BLK : (b + 1) * BLK] = (x + y).astype(BF16)
        return carry

    lax.fori_loop(0, leaves, leaf, 0)


def extend(child_map, child_samples, leaves):
    samples_here, rows_group = child_samples.shape[2:]
    return pl.pallas_call(
        extend_kernel,
        out_shape=jax.ShapeDtypeStruct((leaves, 2, samples_here, rows_group // leaves), BF16),
        in_specs=[
            pl.BlockSpec(memory_space=pltpu.SMEM),
            pl.BlockSpec(memory_space=pltpu.VMEM),
        ],
        out_specs=pl.BlockSpec(memory_space=pltpu.VMEM),
        compiler_params=params(),
        cost_estimate=pl.CostEstimate(flops=1 << 20, bytes_accessed=3 << 20, transcendentals=0),
        name="extend",
    )(child_map, child_samples)


def adjoint_kernel(pattern_ref, probe_ref, sparse_ref, above_ref, own_ref, below_ref, acc):
    b = pl.program_id(0)

    @pl.when(b == 0)
    def _():
        acc[...] = jnp.zeros_like(acc)

    probe = probe_ref[...]
    for s in range(0, 3 * SLOTS, 2):
        pair = jnp.concatenate([sparse_ref[0, s], sparse_ref[0, s + 1]], axis=1)
        product = jnp.dot(probe, pair, preferred_element_type=F32)
        for i in range(2):
            target = pattern_ref[b, s + i]
            acc[s // SLOTS, target] += product[:, i * BLK : (i + 1) * BLK]

    @pl.when(b == pl.num_programs(0) - 1)
    def _():
        above_ref[...] = acc[0].astype(BF16)
        own_ref[...] = acc[1]
        below_ref[...] = acc[2].astype(BF16)


def adjoint(pattern, probe, sparse):
    blocks = sparse.shape[0]
    shape = (blocks, S, BLK)
    whole = pl.BlockSpec(shape, lambda b: (0, 0, 0))
    return pl.pallas_call(
        adjoint_kernel,
        grid=(blocks,),
        out_shape=[
            jax.ShapeDtypeStruct(shape, BF16),
            jax.ShapeDtypeStruct(shape, F32),
            jax.ShapeDtypeStruct(shape, BF16),
        ],
        in_specs=[
            pl.BlockSpec(memory_space=pltpu.SMEM),
            pl.BlockSpec((S, BLK), lambda b: (0, b)),
            pl.BlockSpec((1, 3 * SLOTS, BLK, BLK), lambda b: (b, 0, 0, 0)),
        ],
        out_specs=[whole, whole, whole],
        scratch_shapes=[pltpu.VMEM((3,) + shape, F32)],
        compiler_params=params(),
        cost_estimate=pl.CostEstimate(flops=4 << 30, bytes_accessed=8 << 20, transcendentals=0),
        name="adjoint",
    )(pattern, probe, sparse)


def forward_kernel(pattern_ref, before_ref, own_ref, after_ref, sparse_ref, out_ref):
    b = pl.program_id(0)
    regions = (before_ref, own_ref, after_ref)
    taken = []
    for s in range(3 * SLOTS):
        start = pl.multiple_of(pattern_ref[b, s] * BLK, BLK)
        taken.append(regions[s // SLOTS][:, pl.ds(start, BLK)])
    left = jnp.concatenate(taken, axis=1)
    right = jnp.concatenate([sparse_ref[0, s] for s in range(3 * SLOTS)], axis=1)
    out_ref[...] = lax.dot_general(
        left, right, (((1,), (1,)), ((), ())), preferred_element_type=F32
    )


def forward(pattern, before, own, after, sparse):
    blocks = sparse.shape[0]
    rows = own.shape[1]
    whole = pl.BlockSpec((S, rows), lambda b: (0, 0))
    return pl.pallas_call(
        forward_kernel,
        grid=(blocks,),
        out_shape=jax.ShapeDtypeStruct((S, rows), F32),
        in_specs=[
            pl.BlockSpec(memory_space=pltpu.SMEM),
            whole,
            whole,
            whole,
            pl.BlockSpec((1, 3 * SLOTS, BLK, BLK), lambda b: (b, 0, 0, 0)),
        ],
        out_specs=pl.BlockSpec((S, BLK), lambda b: (0, b)),
        compiler_params=params(),
        cost_estimate=pl.CostEstimate(flops=4 << 30, bytes_accessed=8 << 20, transcendentals=0),
        name="forward",
    )(pattern, before, own, after, sparse)


def gram_kernel(ext_ref, sparse_ref, own_ref, down_ref, up_ref, samples_ref, gram_ref, sent_ref):
    step = pl.program_id(0)
    width = samples_ref.shape[2]

    @pl.when(step == 0)
    def _():
        gram_ref[...] = jnp.zeros_like(gram_ref)

    for k in range(2):
        y = ext_ref[:, k].reshape(S, width).astype(F32)
        if k == 0:
            y += sparse_ref[...]
        else:
            parts = []
            for c in range(width // BLK):
                parts.append(own_ref[c] + down_ref[c].astype(F32) + up_ref[c].astype(F32))
            y += jnp.concatenate(parts, axis=1)
        samples_ref[k] = y
        gram_ref[k] += lax.dot_general(
            y, y, (((1,), (1,)), ((), ())), precision=HIGHEST, preferred_element_type=F32
        )

    @pl.when(step == pl.num_programs(0) - 1)
    def _():
        sent_ref[...] = gram_ref[...].astype(BF16)


def gram(ext, sparse, own, down, up):
    rows = sparse.shape[1]
    width = 2 * BLK
    leaves, _, here, _ = ext.shape
    terms = pl.BlockSpec((width // BLK, S, BLK), lambda i: (i, 0, 0))
    whole = pl.BlockSpec((2, S, S), lambda i: (0, 0, 0))
    return pl.pallas_call(
        gram_kernel,
        grid=(rows // width,),
        out_shape=[
            jax.ShapeDtypeStruct((2, S, rows), F32),
            jax.ShapeDtypeStruct((2, S, S), F32),
            jax.ShapeDtypeStruct((2, S, S), BF16),
        ],
        in_specs=[
            pl.BlockSpec((leaves, 2, here, width), lambda i: (0, 0, 0, i)),
            pl.BlockSpec((S, width), lambda i: (0, i)),
            terms,
            terms,
            terms,
        ],
        out_specs=[pl.BlockSpec((2, S, width), lambda i: (0, 0, i)), whole, whole],
        compiler_params=params(),
        cost_estimate=pl.CostEstimate(flops=2 << 30, bytes_accessed=7 << 20, transcendentals=0),
        name="gram",
    )(ext, sparse, own, down, up)


def factorize(work, count):
    lane = lax.broadcasted_iota(jnp.int32, (8, BLK), 1)
    for lo in range(0, S, PANEL):
        half = lo // BLK
        rows = [
            [work[b][pl.ds(lo + i, 8, stride=PITCH), :] for b in range(2)] for i in range(PANEL)
        ]
        for j in range(PANEL):
            at = lo + j - half * BLK
            row = rows[j]
            scale = lax.rsqrt(jnp.broadcast_to(row[half][:, at : at + 1], (8, BLK)))
            here = lane == at
            done = [x * scale for x in row]
            done[half] = jnp.where(here, scale, done[half])
            rows[j] = done
            for i in range(j + 1, PANEL):
                to = at + i - j
                factor = jnp.broadcast_to(row[half][:, to : to + 1], (8, BLK)) * scale
                new = []
                for b in range(2):
                    base = rows[i][b]
                    if b == half:
                        base = jnp.where(here, 0.0, base)
                    new.append(base - factor * done[b])
                rows[i] = new
        for i in range(PANEL):
            for b in range(2):
                work[b][pl.ds(lo + i, 8, stride=PITCH), :] = rows[i][b]
        end = lo + PANEL
        if end == S:
            break
        row_id = lax.broadcasted_iota(jnp.int32, (PANEL, BLK), 0) + lo
        col_id = lax.broadcasted_iota(jnp.int32, (PANEL, BLK), 1) + BLK * half
        dead = (col_id > row_id) & (col_id < end)
        cols = lax.broadcasted_iota(jnp.int32, (S - end, BLK), 1) + BLK * half
        mine = (cols >= lo) & (cols < end)
        for m in range(count):
            base = m * PITCH
            panel = [work[b][base + lo : base + end, :] for b in range(2)]
            masked = [jnp.where(dead, 0.0, x) if b == half else x for b, x in enumerate(panel)]
            skip = end // BLK
            left = panel[1] if skip else jnp.concatenate(panel, axis=1)
            lh, lm, ll = split3(left)
            rh, rm, rl = split3(jnp.concatenate(masked, axis=1))
            product = lax.dot_general(
                jnp.concatenate([lh, lh, lm, lh, ll, lm], axis=0),
                jnp.concatenate([rh, rm, rh, rl, rh, rm], axis=0),
                (((0,), (0,)), ((), ())),
                preferred_element_type=F32,
            )[end - skip * BLK :]
            for b in range(2):
                old = work[b][base + end : base + S, :]
                if b == half:
                    old = jnp.where(mine, 0.0, old)
                work[b][base + end : base + S, :] = old - product[:, b * BLK : (b + 1) * BLK]


def factor_kernel(g0_ref, g1_ref, g2_ref, samples_ref, row_ref, col_ref, transfer_ref, w0, w1):
    work = (w0, w1)
    grams = (g0_ref, g1_ref, g2_ref)
    for m in range(8):
        source = grams[m // 2 % 3]
        for b in range(2):
            work[b][m * PITCH : m * PITCH + S, :] = source[m % 2, :, b * BLK : (b + 1) * BLK]
    factorize(work, 6)
    row_id = lax.broadcasted_iota(jnp.int32, (S, S), 0)
    col_id = lax.broadcasted_iota(jnp.int32, (S, S), 1)

    def read(m):
        return jnp.concatenate(
            [work[b][m * PITCH : m * PITCH + S, :] for b in range(2)], axis=1
        )

    gain = math.sqrt(samples_ref.shape[2])
    for k in range(2):
        found = [read(2 * level + k) for level in range(3)]
        inverse = [jnp.where(col_id <= row_id, x, 0.0) for x in found]
        upper = [
            jnp.where(col_id > row_id, x, jnp.where(col_id == row_id, 1.0 / x, 0.0))
            for x in found[:2]
        ]
        basis = dot3(inverse[0], samples_ref[k], ((1,), (0,))) * gain
        (row_ref, col_ref)[k][...] = basis.astype(BF16)
        for level in range(2):
            transfer_ref[k, level] = dot3(upper[level], inverse[level + 1], ((1,), (1,)))


def factor(g0, g1, g2, samples):
    rows = samples.shape[2]
    vmem = pl.BlockSpec(memory_space=pltpu.VMEM)
    return pl.pallas_call(
        factor_kernel,
        out_shape=[
            jax.ShapeDtypeStruct((S, rows), BF16),
            jax.ShapeDtypeStruct((S, rows), BF16),
            jax.ShapeDtypeStruct((2, 2, S, S), F32),
        ],
        in_specs=[vmem] * 4,
        out_specs=[vmem] * 3,
        scratch_shapes=[pltpu.VMEM((8 * PITCH, BLK), F32)] * 2,
        compiler_params=params(),
        name="factor",
    )(g0, g1, g2, samples)


def shifted(block, axis, distance):
    devices = range(lax.axis_size(axis))
    route = [(i - distance, i) for i in devices if i - distance in devices]
    return lax.ppermute(block, axis, route)


def from_partner(value, axis, bit):
    mask = 2**bit
    pairs = [(source, source ^ mask) for source in range(lax.axis_size(axis))]
    return lax.ppermute(value, axis, pairs)


def local(
    child_samples, child_map, forward_probe, adjoint_probe, stored_sparse_blocks, block_pattern
):
    leaves = lax.axis_size("col")
    row_pos = lax.axis_index("row")
    before = shifted(forward_probe, "row", 1)
    after = shifted(forward_probe, "row", -1)
    pattern = lax.dynamic_index_in_dim(block_pattern, row_pos, 0, keepdims=False)
    sent = extend(child_map, child_samples, leaves)
    ext = lax.all_to_all(sent, "col", split_axis=0, concat_axis=0, tiled=True)
    above, own, below = adjoint(pattern, adjoint_probe, stored_sparse_blocks)
    down = shifted(above, "row", -1)
    up = shifted(below, "row", 1)
    sparse = forward(pattern, before, forward_probe, after, stored_sparse_blocks)
    samples, g0, g0_sent = gram(ext, sparse, own, down, up)
    g1 = g0 + from_partner(g0_sent, "col", 0).astype(F32)
    g2 = g1 + from_partner(g1.astype(BF16), "col", 1).astype(F32)
    return tuple(factor(g0, g1, g2, samples))


def solution(mesh):
    return jax.shard_map(
        local,
        mesh=mesh,
        in_specs=(
            P(None, None, "col", "row"),
            P(None, "row"),
            P(None, ("row", "col")),
            P(None, ("row", "col")),
            P(("row", "col"), None, None, None),
            P(None, "col", None),
        ),
        out_specs=(
            P(None, ("row", "col")),
            P(None, ("row", "col")),
            P(None, None, ("row", "col"), None),
        ),
        check_vma=False,
    )
```

```python
import math

import jax
import jax.numpy as jnp
from jax import lax
from jax.experimental import pallas as pl
from jax.experimental.pallas import tpu as pltpu
from jax.sharding import PartitionSpec as P

S = 256
BLK = 128
SLOTS = 6
PANEL = 32
PITCH = S + 8
F32 = jnp.float32
BF16 = jnp.bfloat16
MESH = pl.DeviceIdType.MESH
VMEM_LIMIT = 56 << 20


def params():
    return pltpu.CompilerParams(vmem_limit_bytes=VMEM_LIMIT)


def split3(x):
    high = x.astype(BF16)
    rest = x - high.astype(F32)
    mid = rest.astype(BF16)
    low = (rest - mid.astype(F32)).astype(BF16)
    return high, mid, low


def dot3(a, b, dims):
    ah, am, _ = split3(a)
    bh, bm, _ = split3(b)
    dn = (dims, ((), ()))
    out = lax.dot_general(ah, bh, dn, preferred_element_type=F32)
    out += lax.dot_general(ah, bm, dn, preferred_element_type=F32)
    out += lax.dot_general(am, bh, dn, preferred_element_type=F32)
    return out


def terms_kernel(
    pattern_ref, map_ref, probe_ref, forward_ref, sparse_ref, child_ref,
    sent_ref, above_ref, own_ref, below_ref, blocked_ref,
    acc0, acc1, acc2, child, child_sem,
):
    b = pl.program_id(0)
    steps = pl.num_programs(0)
    accs = (acc0, acc1, acc2)
    fetch = pltpu.make_async_copy(child_ref, child, child_sem)

    @pl.when(b == 0)
    def _():
        fetch.start()
        for acc in accs:
            acc[...] = jnp.zeros_like(acc)

    blocked_ref[0] = forward_ref[...]
    probe = probe_ref[...]
    for s in range(0, SLOTS, 2):
        for q in range(3):
            slot = q * SLOTS + s
            pair = jnp.concatenate([sparse_ref[0, slot], sparse_ref[0, slot + 1]], axis=1)
            product = jnp.dot(probe, pair, preferred_element_type=F32)
            for i in range(2):
                target = pattern_ref[b, slot + i]
                accs[q][target] += product[:, i * BLK : (i + 1) * BLK]

    leaves = sent_ref.shape[0]
    blocks = sent_ref.shape[3] // BLK
    first_step = 4
    share = leaves // 4

    @pl.when(b == first_step)
    def _():
        fetch.wait()

    @pl.when(b >= first_step)
    def _():
        def leaf(i, carry):
            d = (b - first_step) * share + i
            for c in range(blocks):
                first = pl.multiple_of(map_ref[0, d * blocks + c] * BLK, BLK)
                second = pl.multiple_of(map_ref[1, d * blocks + c] * BLK, BLK)
                for k in range(2):
                    x = child[0, k, :, pl.ds(first, BLK)].astype(F32)
                    y = child[1, k, :, pl.ds(second, BLK)].astype(F32)
                    sent_ref[d, k, :, c * BLK : (c + 1) * BLK] = (x + y).astype(BF16)
            return carry

        lax.fori_loop(0, share, leaf, 0)

    @pl.when(b == steps - 1)
    def _():
        above_ref[...] = acc0[...].astype(BF16)
        own_ref[...] = acc1[...]
        below_ref[...] = acc2[...].astype(BF16)


def local_terms(pattern, child_map, probe, forward_probe, sparse, child_samples, leaves):
    blocks = sparse.shape[0]
    samples_here, rows_group = child_samples.shape[2:]
    shape = (blocks, S, BLK)
    sent = (leaves, 2, samples_here, rows_group // leaves)
    whole = pl.BlockSpec(shape, lambda b: (0, 0, 0))
    smem = pl.BlockSpec(memory_space=pltpu.SMEM)
    return pl.pallas_call(
        terms_kernel,
        grid=(blocks,),
        out_shape=[
            jax.ShapeDtypeStruct(sent, BF16),
            jax.ShapeDtypeStruct(shape, BF16),
            jax.ShapeDtypeStruct(shape, F32),
            jax.ShapeDtypeStruct(shape, BF16),
            jax.ShapeDtypeStruct(shape, BF16),
        ],
        in_specs=[
            smem,
            smem,
            pl.BlockSpec((S, BLK), lambda b: (0, b)),
            pl.BlockSpec((S, BLK), lambda b: (0, b)),
            pl.BlockSpec((1, 3 * SLOTS, BLK, BLK), lambda b: (b, 0, 0, 0)),
            pl.BlockSpec(memory_space=pl.ANY),
        ],
        out_specs=[pl.BlockSpec(sent, lambda b: (0, 0, 0, 0)), whole, whole, whole]
        + [pl.BlockSpec((1, S, BLK), lambda b: (b, 0, 0))],
        scratch_shapes=[pltpu.VMEM(shape, F32)] * 3
        + [pltpu.VMEM(child_samples.shape, BF16), pltpu.SemaphoreType.DMA],
        compiler_params=params(),
        name="terms",
    )(pattern, child_map, probe, forward_probe, sparse, child_samples)


def exchange_kernel(
    pattern_ref, probe_ref, sent_ref, above_ref, own_ref, below_ref, sparse_ref,
    samples_ref, gram_ref,
    ext, before, after, down, up, own, blocks, samples, gram, packed, partner,
    ext_send, ext_recv, row_send, row_recv, quad_send, quad_recv, local_sem, block_sem,
):
    row = lax.axis_index("row")
    col = lax.axis_index("col")
    n_row = lax.axis_size("row")
    n_col = lax.axis_size("col")
    n_blocks = blocks.shape[0]
    side = 4
    cx = col // side
    cy = col % side
    inner_up = row < n_row - 1
    inner_down = row > 0

    peers = []
    for d in range(1, n_col):
        px = (cx + d // side) % side
        py = (cy + d % side) % side
        peers.append(px * side + py)

    barrier = pltpu.get_barrier_semaphore()
    for peer in peers:
        pl.semaphore_signal(barrier, inc=1, device_id=(row, peer), device_id_type=MESH)

    for neighbour in ((row + 1) % n_row, (row + n_row - 1) % n_row):
        pl.semaphore_signal(barrier, inc=1, device_id=(neighbour, col), device_id_type=MESH)

    fetches = [
        pltpu.make_async_copy(sparse_ref.at[b], blocks.at[b], block_sem.at[b])
        for b in range(n_blocks)
    ]
    own_fetch = pltpu.make_async_copy(own_ref, own, local_sem.at[0])
    ext_fetch = pltpu.make_async_copy(sent_ref.at[col], ext.at[col], local_sem.at[1])
    for fetch in fetches:
        fetch.start()
    own_fetch.start()
    ext_fetch.start()

    @pl.when(row == 0)
    def _():
        before[...] = jnp.zeros_like(before)
        up[...] = jnp.zeros_like(up)

    @pl.when(row == n_row - 1)
    def _():
        after[...] = jnp.zeros_like(after)
        down[...] = jnp.zeros_like(down)

    def to_row(source, target, index, step):
        return pltpu.make_async_remote_copy(
            src_ref=source,
            dst_ref=target,
            send_sem=row_send.at[index],
            recv_sem=row_recv.at[index],
            device_id=(row + step, col),
            device_id_type=MESH,
        )

    rising = [to_row(probe_ref, before, 0, 1), to_row(below_ref, up, 1, 1)]
    falling = [to_row(probe_ref, after, 2, -1), to_row(above_ref, down, 3, -1)]

    pl.semaphore_wait(barrier, n_col + 1)

    @pl.when(inner_up)
    def _():
        rising[0].start()

    @pl.when(inner_down)
    def _():
        falling[0].start()

    spread = [
        pltpu.make_async_remote_copy(
            src_ref=sent_ref.at[peer],
            dst_ref=ext.at[col],
            send_sem=ext_send.at[i],
            recv_sem=ext_recv.at[i],
            device_id=(row, peer),
            device_id_type=MESH,
        )
        for i, peer in enumerate(peers)
    ]
    for copy in spread:
        copy.start()

    @pl.when(inner_up)
    def _():
        rising[1].start()

    @pl.when(inner_down)
    def _():
        falling[1].start()

    def product(b, regions):
        left = []
        right = []
        for q, source in regions:
            for s in range(q * SLOTS, (q + 1) * SLOTS):
                left.append(source[pattern_ref[b, s]])
                right.append(blocks[b, s])
        return lax.dot_general(
            jnp.concatenate(left, axis=1),
            jnp.concatenate(right, axis=1),
            (((1,), (1,)), ((), ())),
            preferred_element_type=F32,
        )

    for fetch in fetches:
        fetch.wait()

    def own_region(b, carry):
        lanes = pl.ds(pl.multiple_of(b * BLK, BLK), BLK)
        samples[0, :, lanes] = product(b, [(1, probe_ref)])
        return carry

    lax.fori_loop(0, n_blocks, own_region, 0)

    @pl.when(inner_down)
    def _():
        rising[0].wait_recv()

    @pl.when(inner_up)
    def _():
        falling[0].wait_recv()

    def other_regions(b, carry):
        lanes = pl.ds(pl.multiple_of(b * BLK, BLK), BLK)
        samples[0, :, lanes] += product(b, [(0, before), (2, after)])
        return carry

    lax.fori_loop(0, n_blocks, other_regions, 0)

    gram[...] = jnp.zeros_like(gram)
    own_fetch.wait()
    ext_fetch.wait()
    for copy in spread:
        copy.wait_recv()

    @pl.when(inner_down)
    def _():
        rising[1].wait_recv()

    @pl.when(inner_up)
    def _():
        falling[1].wait_recv()

    def assemble(h, carry):
        lanes = pl.ds(pl.multiple_of(h * 2 * BLK, 2 * BLK), 2 * BLK)
        for k in range(2):
            y = ext[:, k, :, lanes].reshape(S, 2 * BLK).astype(F32)
            if k == 0:
                y += samples[0, :, lanes]
            else:
                parts = []
                for c in range(2):
                    at = h * 2 + c
                    parts.append(own[at] + down[at].astype(F32) + up[at].astype(F32))
                y += jnp.concatenate(parts, axis=1)
            samples[k, :, lanes] = y
            gram[k] += dot3(y, y, ((1,), (1,)))
        return carry

    lax.fori_loop(0, n_blocks // 2, assemble, 0)

    row_id = lax.broadcasted_iota(jnp.int32, (BLK, BLK), 0)
    col_id = lax.broadcasted_iota(jnp.int32, (BLK, BLK), 1)
    for k in range(2):
        last = gram[k, BLK:, BLK:]
        diagonal = jnp.sum(jnp.where(row_id == col_id, last, 0.0), axis=0, keepdims=True)
        pieces = (
            (0, gram[k, :BLK, BLK:]),
            (BLK, jnp.where(col_id >= row_id, gram[k, :BLK, :BLK], last)),
            (2 * BLK, jnp.broadcast_to(diagonal, (16, BLK))),
        )
        for at, piece in pieces:
            gram_ref[0, k, at : at + piece.shape[0]] = piece
            packed[k, at : at + piece.shape[0]] = piece.astype(BF16)

    quad = [
        pltpu.make_async_remote_copy(
            src_ref=packed,
            dst_ref=partner.at[i],
            send_sem=quad_send.at[i],
            recv_sem=quad_recv.at[i],
            device_id=(row, cx * side + other),
            device_id_type=MESH,
        )
        for i, other in enumerate(
            (cy + 1 - 2 * (cy % 2), (cy + 2) % side, side - 1 - cy)
        )
    ]
    for copy in quad:
        copy.start()
    store = pltpu.make_async_copy(samples, samples_ref, local_sem.at[2])
    store.start()

    @pl.when(inner_up)
    def _():
        for copy in rising:
            copy.wait_send()

    @pl.when(inner_down)
    def _():
        for copy in falling:
            copy.wait_send()

    for copy in spread:
        copy.wait_send()
    quad[0].wait_recv()
    for k in range(2):
        gram_ref[1, k] = gram_ref[0, k] + partner[0, k].astype(F32)
    quad[1].wait_recv()
    quad[2].wait_recv()
    for k in range(2):
        gram_ref[2, k] = gram_ref[1, k] + partner[1, k].astype(F32) + partner[2, k].astype(F32)
    for copy in quad:
        copy.wait_send()
    store.wait()


def exchange(pattern, probe, sent, above, own, below, sparse):
    rows = sent.shape[3]
    leaves = sent.shape[0]
    held = 2 * BLK + 16
    anywhere = pl.BlockSpec(memory_space=pl.ANY)
    vmem = pl.BlockSpec(memory_space=pltpu.VMEM)
    dma = pltpu.SemaphoreType.DMA
    return pl.pallas_call(
        exchange_kernel,
        out_shape=[
            jax.ShapeDtypeStruct((2, S, rows), F32),
            jax.ShapeDtypeStruct((3, 2, held, BLK), F32),
        ],
        in_specs=[pl.BlockSpec(memory_space=pltpu.SMEM), vmem] + [anywhere] * 5,
        out_specs=[anywhere, vmem],
        scratch_shapes=[
            pltpu.VMEM(sent.shape, BF16),
            pltpu.VMEM(probe.shape, BF16),
            pltpu.VMEM(probe.shape, BF16),
            pltpu.VMEM(above.shape, BF16),
            pltpu.VMEM(below.shape, BF16),
            pltpu.VMEM(own.shape, F32),
            pltpu.VMEM(sparse.shape, BF16),
            pltpu.VMEM((2, S, rows), F32),
            pltpu.VMEM((2, S, S), F32),
            pltpu.VMEM((2, held, BLK), BF16),
            pltpu.VMEM((3, 2, held, BLK), BF16),
            dma((leaves - 1,)),
            dma((leaves - 1,)),
            dma((4,)),
            dma((4,)),
            dma((3,)),
            dma((3,)),
            dma((3,)),
            dma((sparse.shape[0],)),
        ],
        compiler_params=pltpu.CompilerParams(
            collective_id=0, has_side_effects=True, vmem_limit_bytes=VMEM_LIMIT
        ),
        name="exchange",
    )(pattern, probe, sent, above, own, below, sparse)


def factorize(work, count):
    lane = lax.broadcasted_iota(jnp.int32, (8, BLK), 1)
    for lo in range(0, S, PANEL):
        half = lo // BLK
        rows = [
            [work[b][pl.ds(lo + i, 8, stride=PITCH), :] for b in range(2)] for i in range(PANEL)
        ]
        for j in range(PANEL):
            at = lo + j - half * BLK
            row = rows[j]
            scale = lax.rsqrt(jnp.broadcast_to(row[half][:, at : at + 1], (8, BLK)))
            here = lane == at
            done = [x * scale for x in row]
            done[half] = jnp.where(here, scale, done[half])
            rows[j] = done
            for i in range(j + 1, PANEL):
                to = at + i - j
                factor = jnp.broadcast_to(row[half][:, to : to + 1], (8, BLK)) * scale
                new = []
                for b in range(2):
                    base = rows[i][b]
                    if b == half:
                        base = jnp.where(here, 0.0, base)
                    new.append(base - factor * done[b])
                rows[i] = new
        for i in range(PANEL):
            for b in range(2):
                work[b][pl.ds(lo + i, 8, stride=PITCH), :] = rows[i][b]
        end = lo + PANEL
        if end == S:
            break
        row_id = lax.broadcasted_iota(jnp.int32, (PANEL, BLK), 0) + lo
        col_id = lax.broadcasted_iota(jnp.int32, (PANEL, BLK), 1) + BLK * half
        dead = (col_id > row_id) & (col_id < end)
        cols = lax.broadcasted_iota(jnp.int32, (S - end, BLK), 1) + BLK * half
        mine = (cols >= lo) & (cols < end)
        for m in range(count):
            base = m * PITCH
            panel = [work[b][base + lo : base + end, :] for b in range(2)]
            masked = [jnp.where(dead, 0.0, x) if b == half else x for b, x in enumerate(panel)]
            skip = end // BLK
            left = panel[1] if skip else jnp.concatenate(panel, axis=1)
            lh, lm, ll = split3(left)
            rh, rm, rl = split3(jnp.concatenate(masked, axis=1))
            product = lax.dot_general(
                jnp.concatenate([lh, lh, lm, lh, ll, lm], axis=0),
                jnp.concatenate([rh, rm, rh, rl, rh, rm], axis=0),
                (((0,), (0,)), ((), ())),
                preferred_element_type=F32,
            )[end - skip * BLK :]
            for b in range(2):
                old = work[b][base + end : base + S, :]
                if b == half:
                    old = jnp.where(mine, 0.0, old)
                work[b][base + end : base + S, :] = old - product[:, b * BLK : (b + 1) * BLK]


def factor_kernel(gram_ref, samples_ref, row_ref, col_ref, transfer_ref, w0, w1):
    work = (w0, w1)
    corner_row = lax.broadcasted_iota(jnp.int32, (BLK, BLK), 0)
    corner_col = lax.broadcasted_iota(jnp.int32, (BLK, BLK), 1)
    for m in range(8):
        held = gram_ref.at[m // 2 % 3, m % 2]
        shared = held[BLK : 2 * BLK]
        at = m * PITCH
        w0[at : at + BLK, :] = shared
        w1[at : at + BLK, :] = held[:BLK]
        w1[at + BLK : at + S, :] = jnp.where(
            corner_row == corner_col,
            jnp.broadcast_to(held[2 * BLK : 2 * BLK + 1], (BLK, BLK)),
            shared.T,
        )
        w0[at + BLK : at + S, :] = jnp.zeros((BLK, BLK), F32)
    factorize(work, 6)
    row_id = lax.broadcasted_iota(jnp.int32, (S, S), 0)
    col_id = lax.broadcasted_iota(jnp.int32, (S, S), 1)

    def read(m):
        return jnp.concatenate(
            [work[b][m * PITCH : m * PITCH + S, :] for b in range(2)], axis=1
        )

    gain = math.sqrt(samples_ref.shape[2])
    for k in range(2):
        found = [read(2 * level + k) for level in range(3)]
        inverse = [jnp.where(col_id <= row_id, x, 0.0) for x in found]
        upper = [
            jnp.where(col_id > row_id, x, jnp.where(col_id == row_id, 1.0 / x, 0.0))
            for x in found[:2]
        ]
        basis = dot3(inverse[0], samples_ref[k], ((1,), (0,))) * gain
        (row_ref, col_ref)[k][...] = basis.astype(BF16)
        for level in range(2):
            transfer_ref[k, level] = dot3(upper[level], inverse[level + 1], ((1,), (1,)))


def factor(grams, samples):
    rows = samples.shape[2]
    vmem = pl.BlockSpec(memory_space=pltpu.VMEM)
    return pl.pallas_call(
        factor_kernel,
        out_shape=[
            jax.ShapeDtypeStruct((S, rows), BF16),
            jax.ShapeDtypeStruct((S, rows), BF16),
            jax.ShapeDtypeStruct((2, 2, S, S), F32),
        ],
        in_specs=[vmem] * 2,
        out_specs=[vmem] * 3,
        scratch_shapes=[pltpu.VMEM((8 * PITCH, BLK), F32)] * 2,
        compiler_params=params(),
        name="factor",
    )(grams, samples)


def local(
    child_samples, child_map, forward_probe, adjoint_probe, stored_sparse_blocks, block_pattern
):
    leaves = lax.axis_size("col")
    row_pos = lax.axis_index("row")
    pattern = lax.dynamic_index_in_dim(block_pattern, row_pos, 0, keepdims=False)
    sent, above, own, below, blocked = local_terms(
        pattern, child_map, adjoint_probe, forward_probe, stored_sparse_blocks, child_samples, leaves
    )
    samples, grams = exchange(
        pattern, blocked, sent, above, own, below, stored_sparse_blocks
    )
    return tuple(factor(grams, samples))


def solution(mesh):
    return jax.shard_map(
        local,
        mesh=mesh,
        in_specs=(
            P(None, None, "col", "row"),
            P(None, "row"),
            P(None, ("row", "col")),
            P(None, ("row", "col")),
            P(("row", "col"), None, None, None),
            P(None, "col", None),
        ),
        out_specs=(
            P(None, ("row", "col")),
            P(None, ("row", "col")),
            P(None, None, ("row", "col"), None),
        ),
        check_vma=False,
    )
```

```python
import math

import jax
import jax.numpy as jnp
from jax import lax
from jax.experimental import pallas as pl
from jax.experimental.pallas import tpu as pltpu
from jax.sharding import PartitionSpec as P

S = 256
BLK = 128
SLOTS = 6
PANEL = 16
SUB = 8
PITCH = S + 8
F32 = jnp.float32
BF16 = jnp.bfloat16
MESH = pl.DeviceIdType.MESH
VMEM_LIMIT = 56 << 20


def params():
    return pltpu.CompilerParams(vmem_limit_bytes=VMEM_LIMIT)


def split3(x):
    high = x.astype(BF16)
    rest = x - high.astype(F32)
    mid = rest.astype(BF16)
    low = (rest - mid.astype(F32)).astype(BF16)
    return high, mid, low


def dot3(a, b, dims):
    ah, am, _ = split3(a)
    bh, bm, _ = split3(b)
    dn = (dims, ((), ()))
    out = lax.dot_general(ah, bh, dn, preferred_element_type=F32)
    out += lax.dot_general(ah, bm, dn, preferred_element_type=F32)
    out += lax.dot_general(am, bh, dn, preferred_element_type=F32)
    return out


def terms_kernel(
    pattern_ref, map_ref, probe_ref, forward_ref, sparse_ref, child_ref,
    sent_ref, above_ref, own_ref, below_ref, blocked_ref,
    acc0, acc1, acc2, child, child_sem,
):
    b = pl.program_id(0)
    steps = pl.num_programs(0)
    accs = (acc0, acc1, acc2)
    fetch = pltpu.make_async_copy(child_ref, child, child_sem)

    @pl.when(b == 0)
    def _():
        fetch.start()
        for acc in accs:
            acc[...] = jnp.zeros_like(acc)

    blocked_ref[0] = forward_ref[...]
    probe = probe_ref[...]
    for s in range(0, SLOTS, 2):
        for q in range(3):
            slot = q * SLOTS + s
            pair = jnp.concatenate([sparse_ref[0, slot], sparse_ref[0, slot + 1]], axis=1)
            product = jnp.dot(probe, pair, preferred_element_type=F32)
            for i in range(2):
                target = pattern_ref[b, slot + i]
                accs[q][target] += product[:, i * BLK : (i + 1) * BLK]

    leaves = sent_ref.shape[0]
    blocks = sent_ref.shape[3] // BLK
    first_step = 4
    share = leaves // 4

    @pl.when(b == first_step)
    def _():
        fetch.wait()

    @pl.when(b >= first_step)
    def _():
        def leaf(i, carry):
            d = (b - first_step) * share + i
            for c in range(blocks):
                first = pl.multiple_of(map_ref[0, d * blocks + c] * BLK, BLK)
                second = pl.multiple_of(map_ref[1, d * blocks + c] * BLK, BLK)
                for k in range(2):
                    x = child[0, k, :, pl.ds(first, BLK)].astype(F32)
                    y = child[1, k, :, pl.ds(second, BLK)].astype(F32)
                    sent_ref[d, k, :, c * BLK : (c + 1) * BLK] = (x + y).astype(BF16)
            return carry

        lax.fori_loop(0, share, leaf, 0)

    @pl.when(b == steps - 1)
    def _():
        above_ref[...] = acc0[...].astype(BF16)
        own_ref[...] = acc1[...]
        below_ref[...] = acc2[...].astype(BF16)


def local_terms(pattern, child_map, probe, forward_probe, sparse, child_samples, leaves):
    blocks = sparse.shape[0]
    samples_here, rows_group = child_samples.shape[2:]
    shape = (blocks, S, BLK)
    sent = (leaves, 2, samples_here, rows_group // leaves)
    whole = pl.BlockSpec(shape, lambda b: (0, 0, 0))
    smem = pl.BlockSpec(memory_space=pltpu.SMEM)
    return pl.pallas_call(
        terms_kernel,
        grid=(blocks,),
        out_shape=[
            jax.ShapeDtypeStruct(sent, BF16),
            jax.ShapeDtypeStruct(shape, BF16),
            jax.ShapeDtypeStruct(shape, F32),
            jax.ShapeDtypeStruct(shape, BF16),
            jax.ShapeDtypeStruct(shape, BF16),
        ],
        in_specs=[
            smem,
            smem,
            pl.BlockSpec((S, BLK), lambda b: (0, b)),
            pl.BlockSpec((S, BLK), lambda b: (0, b)),
            pl.BlockSpec((1, 3 * SLOTS, BLK, BLK), lambda b: (b, 0, 0, 0)),
            pl.BlockSpec(memory_space=pl.ANY),
        ],
        out_specs=[pl.BlockSpec(sent, lambda b: (0, 0, 0, 0)), whole, whole, whole]
        + [pl.BlockSpec((1, S, BLK), lambda b: (b, 0, 0))],
        scratch_shapes=[pltpu.VMEM(shape, F32)] * 3
        + [pltpu.VMEM(child_samples.shape, BF16), pltpu.SemaphoreType.DMA],
        compiler_params=params(),
        name="terms",
    )(pattern, child_map, probe, forward_probe, sparse, child_samples)


def exchange_kernel(
    pattern_ref, probe_ref, sent_ref, above_ref, own_ref, below_ref, sparse_ref,
    samples_ref, gram_ref,
    ext, before, after, down, up, own, blocks, samples, gram, packed, partner,
    ext_send, ext_recv, row_send, row_recv, quad_send, quad_recv, local_sem, block_sem,
):
    row = lax.axis_index("row")
    col = lax.axis_index("col")
    n_row = lax.axis_size("row")
    n_col = lax.axis_size("col")
    n_blocks = blocks.shape[0]
    side = 4
    cx = col // side
    cy = col % side
    inner_up = row < n_row - 1
    inner_down = row > 0

    peers = []
    for d in range(1, n_col):
        px = (cx + d // side) % side
        py = (cy + d % side) % side
        peers.append(px * side + py)

    barrier = pltpu.get_barrier_semaphore()
    for peer in peers:
        pl.semaphore_signal(barrier, inc=1, device_id=(row, peer), device_id_type=MESH)

    for neighbour in ((row + 1) % n_row, (row + n_row - 1) % n_row):
        pl.semaphore_signal(barrier, inc=1, device_id=(neighbour, col), device_id_type=MESH)

    fetches = [
        pltpu.make_async_copy(sparse_ref.at[b], blocks.at[b], block_sem.at[b])
        for b in range(n_blocks)
    ]
    own_fetch = pltpu.make_async_copy(own_ref, own, local_sem.at[0])
    ext_fetch = pltpu.make_async_copy(sent_ref.at[col], ext.at[col], local_sem.at[1])
    for fetch in fetches:
        fetch.start()
    own_fetch.start()
    ext_fetch.start()

    @pl.when(row == 0)
    def _():
        before[...] = jnp.zeros_like(before)
        up[...] = jnp.zeros_like(up)

    @pl.when(row == n_row - 1)
    def _():
        after[...] = jnp.zeros_like(after)
        down[...] = jnp.zeros_like(down)

    def to_row(source, target, index, step):
        return pltpu.make_async_remote_copy(
            src_ref=source,
            dst_ref=target,
            send_sem=row_send.at[index],
            recv_sem=row_recv.at[index],
            device_id=(row + step, col),
            device_id_type=MESH,
        )

    rising = [to_row(probe_ref, before, 0, 1), to_row(below_ref, up, 1, 1)]
    falling = [to_row(probe_ref, after, 2, -1), to_row(above_ref, down, 3, -1)]

    pl.semaphore_wait(barrier, n_col + 1)

    @pl.when(inner_up)
    def _():
        rising[0].start()

    @pl.when(inner_down)
    def _():
        falling[0].start()

    spread = [
        pltpu.make_async_remote_copy(
            src_ref=sent_ref.at[peer],
            dst_ref=ext.at[col],
            send_sem=ext_send.at[i],
            recv_sem=ext_recv.at[i],
            device_id=(row, peer),
            device_id_type=MESH,
        )
        for i, peer in enumerate(peers)
    ]
    for copy in spread:
        copy.start()

    @pl.when(inner_up)
    def _():
        rising[1].start()

    @pl.when(inner_down)
    def _():
        falling[1].start()

    def product(b, regions):
        left = []
        right = []
        for q, source in regions:
            for s in range(q * SLOTS, (q + 1) * SLOTS):
                left.append(source[pattern_ref[b, s]])
                right.append(blocks[b, s])
        return lax.dot_general(
            jnp.concatenate(left, axis=1),
            jnp.concatenate(right, axis=1),
            (((1,), (1,)), ((), ())),
            preferred_element_type=F32,
        )

    for fetch in fetches:
        fetch.wait()

    def own_region(b, carry):
        lanes = pl.ds(pl.multiple_of(b * BLK, BLK), BLK)
        samples[0, :, lanes] = product(b, [(1, probe_ref)])
        return carry

    lax.fori_loop(0, n_blocks, own_region, 0)

    @pl.when(inner_down)
    def _():
        rising[0].wait_recv()

    @pl.when(inner_up)
    def _():
        falling[0].wait_recv()

    def other_regions(b, carry):
        lanes = pl.ds(pl.multiple_of(b * BLK, BLK), BLK)
        samples[0, :, lanes] += product(b, [(0, before), (2, after)])
        return carry

    lax.fori_loop(0, n_blocks, other_regions, 0)

    gram[...] = jnp.zeros_like(gram)
    own_fetch.wait()
    ext_fetch.wait()
    for copy in spread:
        copy.wait_recv()

    @pl.when(inner_down)
    def _():
        rising[1].wait_recv()

    @pl.when(inner_up)
    def _():
        falling[1].wait_recv()

    def assemble(h, carry):
        lanes = pl.ds(pl.multiple_of(h * 2 * BLK, 2 * BLK), 2 * BLK)
        for k in range(2):
            y = ext[:, k, :, lanes].reshape(S, 2 * BLK).astype(F32)
            if k == 0:
                y += samples[0, :, lanes]
            else:
                parts = []
                for c in range(2):
                    at = h * 2 + c
                    parts.append(own[at] + down[at].astype(F32) + up[at].astype(F32))
                y += jnp.concatenate(parts, axis=1)
            samples[k, :, lanes] = y
            gram[k] += dot3(y, y, ((1,), (1,)))
        return carry

    lax.fori_loop(0, n_blocks // 2, assemble, 0)

    row_id = lax.broadcasted_iota(jnp.int32, (BLK, BLK), 0)
    col_id = lax.broadcasted_iota(jnp.int32, (BLK, BLK), 1)
    for k in range(2):
        last = gram[k, BLK:, BLK:]
        diagonal = jnp.sum(jnp.where(row_id == col_id, last, 0.0), axis=0, keepdims=True)
        pieces = (
            (0, gram[k, :BLK, BLK:]),
            (BLK, jnp.where(col_id >= row_id, gram[k, :BLK, :BLK], last)),
            (2 * BLK, jnp.broadcast_to(diagonal, (16, BLK))),
        )
        for at, piece in pieces:
            gram_ref[0, k, at : at + piece.shape[0]] = piece
            packed[k, at : at + piece.shape[0]] = piece.astype(BF16)

    quad = [
        pltpu.make_async_remote_copy(
            src_ref=packed,
            dst_ref=partner.at[i],
            send_sem=quad_send.at[i],
            recv_sem=quad_recv.at[i],
            device_id=(row, cx * side + other),
            device_id_type=MESH,
        )
        for i, other in enumerate(
            (cy + 1 - 2 * (cy % 2), (cy + 2) % side, side - 1 - cy)
        )
    ]
    for copy in quad:
        copy.start()
    store = pltpu.make_async_copy(samples, samples_ref, local_sem.at[2])
    store.start()

    @pl.when(inner_up)
    def _():
        for copy in rising:
            copy.wait_send()

    @pl.when(inner_down)
    def _():
        for copy in falling:
            copy.wait_send()

    for copy in spread:
        copy.wait_send()
    quad[0].wait_recv()
    for k in range(2):
        gram_ref[1, k] = gram_ref[0, k] + partner[0, k].astype(F32)
    quad[1].wait_recv()
    quad[2].wait_recv()
    for k in range(2):
        gram_ref[2, k] = gram_ref[1, k] + partner[1, k].astype(F32) + partner[2, k].astype(F32)
    for copy in quad:
        copy.wait_send()
    store.wait()


def exchange(pattern, probe, sent, above, own, below, sparse):
    rows = sent.shape[3]
    leaves = sent.shape[0]
    held = 2 * BLK + 16
    anywhere = pl.BlockSpec(memory_space=pl.ANY)
    vmem = pl.BlockSpec(memory_space=pltpu.VMEM)
    dma = pltpu.SemaphoreType.DMA
    return pl.pallas_call(
        exchange_kernel,
        out_shape=[
            jax.ShapeDtypeStruct((2, S, rows), F32),
            jax.ShapeDtypeStruct((3, 2, held, BLK), F32),
        ],
        in_specs=[pl.BlockSpec(memory_space=pltpu.SMEM), vmem] + [anywhere] * 5,
        out_specs=[anywhere, vmem],
        scratch_shapes=[
            pltpu.VMEM(sent.shape, BF16),
            pltpu.VMEM(probe.shape, BF16),
            pltpu.VMEM(probe.shape, BF16),
            pltpu.VMEM(above.shape, BF16),
            pltpu.VMEM(below.shape, BF16),
            pltpu.VMEM(own.shape, F32),
            pltpu.VMEM(sparse.shape, BF16),
            pltpu.VMEM((2, S, rows), F32),
            pltpu.VMEM((2, S, S), F32),
            pltpu.VMEM((2, held, BLK), BF16),
            pltpu.VMEM((3, 2, held, BLK), BF16),
            dma((leaves - 1,)),
            dma((leaves - 1,)),
            dma((4,)),
            dma((4,)),
            dma((3,)),
            dma((3,)),
            dma((3,)),
            dma((sparse.shape[0],)),
        ],
        compiler_params=pltpu.CompilerParams(
            collective_id=0, has_side_effects=True, vmem_limit_bytes=VMEM_LIMIT
        ),
        name="exchange",
    )(pattern, probe, sent, above, own, below, sparse)


def splat(x, at):
    return jnp.broadcast_to(x[:, at:at+1], (8, BLK))

def eliminate(rows, first, half, lane):
    count=len(rows)
    for g in range(0, count, SUB):
        base=first+g
        e=[[splat(rows[g+j][half], base+i) if i>=j else None for i in range(SUB)] for j in range(SUB)]
        scale=[]; fac=[]
        for j in range(SUB):
            s=lax.rsqrt(e[j][j]); scale.append(s)
            f=[e[j][i]*s if i>j else None for i in range(SUB)]
            fac.append(f)
            for i in range(j+1,SUB):
                for l in range(i,SUB):
                    e[i][l]=e[i][l]-f[i]*f[l]
        clean=[]
        for j in range(SUB):
            here=lane==base+j
            z=[x*scale[j] for x in rows[g+j]]
            z[half]=jnp.where(here,scale[j],z[half])
            rows[g+j]=z
            for i in range(j+1,SUB):
                r=list(rows[g+i]); r[half]=jnp.where(here,0.0,r[half])
                rows[g+i]=[x-fac[j][i]*y for x,y in zip(r,z)]
            c=list(z); c[half]=jnp.where((lane>base+j)&(lane<base+SUB),0.0,z[half]); clean.append(c)
        for i in range(g+SUB,count):
            r=list(rows[i]); r[half]=jnp.where((lane>=base)&(lane<base+SUB),0.0,r[half])
            for j in range(SUB):
                z=clean[j]
                f=splat(z[half], first+i)
                r=[x-f*y for x,y in zip(r,z)]
            rows[i]=r
    return rows

def factorize(work, count):
    lane = lax.broadcasted_iota(jnp.int32, (8, BLK), 1)
    for lo in range(0, S, PANEL):
        half = lo // BLK
        rows = [
            [work[b][pl.ds(lo + i, 8, stride=PITCH), :] for b in range(2)] for i in range(PANEL)
        ]
        rows = eliminate(rows, lo - half*BLK, half, lane)
        for i in range(PANEL):
            for b in range(2):
                work[b][pl.ds(lo + i, 8, stride=PITCH), :] = rows[i][b]
        end = lo + PANEL
        if end == S:
            break
        row_id = lax.broadcasted_iota(jnp.int32, (PANEL, BLK), 0) + lo
        col_id = lax.broadcasted_iota(jnp.int32, (PANEL, BLK), 1) + BLK * half
        dead = (col_id > row_id) & (col_id < end)
        cols = lax.broadcasted_iota(jnp.int32, (S - end, BLK), 1) + BLK * half
        mine = (cols >= lo) & (cols < end)
        for m in range(count):
            base = m * PITCH
            panel = [work[b][base + lo : base + end, :] for b in range(2)]
            masked = [jnp.where(dead, 0.0, x) if b == half else x for b, x in enumerate(panel)]
            skip = end // BLK
            left = panel[1] if skip else jnp.concatenate(panel, axis=1)
            lh, lm, ll = split3(left)
            rh, rm, rl = split3(jnp.concatenate(masked, axis=1))
            product = lax.dot_general(
                jnp.concatenate([lh, lh, lm, lh, ll, lm], axis=0),
                jnp.concatenate([rh, rm, rh, rl, rh, rm], axis=0),
                (((0,), (0,)), ((), ())),
                preferred_element_type=F32,
            )[end - skip * BLK :]
            for b in range(2):
                old = work[b][base + end : base + S, :]
                if b == half:
                    old = jnp.where(mine, 0.0, old)
                work[b][base + end : base + S, :] = old - product[:, b * BLK : (b + 1) * BLK]


def factor_kernel(gram_ref, samples_ref, row_ref, col_ref, transfer_ref, w0, w1):
    work = (w0, w1)
    corner_row = lax.broadcasted_iota(jnp.int32, (BLK, BLK), 0)
    corner_col = lax.broadcasted_iota(jnp.int32, (BLK, BLK), 1)
    for m in range(8):
        held = gram_ref.at[m // 2 % 3, m % 2]
        shared = held[BLK : 2 * BLK]
        at = m * PITCH
        w0[at : at + BLK, :] = shared
        w1[at : at + BLK, :] = held[:BLK]
        w1[at + BLK : at + S, :] = jnp.where(
            corner_row == corner_col,
            jnp.broadcast_to(held[2 * BLK : 2 * BLK + 1], (BLK, BLK)),
            shared.T,
        )
        w0[at + BLK : at + S, :] = jnp.zeros((BLK, BLK), F32)
    factorize(work, 6)
    row_id = lax.broadcasted_iota(jnp.int32, (S, S), 0)
    col_id = lax.broadcasted_iota(jnp.int32, (S, S), 1)

    def read(m):
        return jnp.concatenate(
            [work[b][m * PITCH : m * PITCH + S, :] for b in range(2)], axis=1
        )

    gain = math.sqrt(samples_ref.shape[2])
    for k in range(2):
        found = [read(2 * level + k) for level in range(3)]
        inverse = [jnp.where(col_id <= row_id, x, 0.0) for x in found]
        upper = [
            jnp.where(col_id > row_id, x, jnp.where(col_id == row_id, 1.0 / x, 0.0))
            for x in found[:2]
        ]
        basis = dot3(inverse[0], samples_ref[k], ((1,), (0,))) * gain
        (row_ref, col_ref)[k][...] = basis.astype(BF16)
        for level in range(2):
            transfer_ref[k, level] = dot3(upper[level], inverse[level + 1], ((1,), (1,)))


def factor(grams, samples):
    rows = samples.shape[2]
    vmem = pl.BlockSpec(memory_space=pltpu.VMEM)
    return pl.pallas_call(
        factor_kernel,
        out_shape=[
            jax.ShapeDtypeStruct((S, rows), BF16),
            jax.ShapeDtypeStruct((S, rows), BF16),
            jax.ShapeDtypeStruct((2, 2, S, S), F32),
        ],
        in_specs=[vmem] * 2,
        out_specs=[vmem] * 3,
        scratch_shapes=[pltpu.VMEM((8 * PITCH, BLK), F32)] * 2,
        compiler_params=params(),
        name="factor",
    )(grams, samples)


def local(
    child_samples, child_map, forward_probe, adjoint_probe, stored_sparse_blocks, block_pattern
):
    leaves = lax.axis_size("col")
    row_pos = lax.axis_index("row")
    pattern = lax.dynamic_index_in_dim(block_pattern, row_pos, 0, keepdims=False)
    sent, above, own, below, blocked = local_terms(
        pattern, child_map, adjoint_probe, forward_probe, stored_sparse_blocks, child_samples, leaves
    )
    samples, grams = exchange(
        pattern, blocked, sent, above, own, below, stored_sparse_blocks
    )
    return tuple(factor(grams, samples))


def solution(mesh):
    return jax.shard_map(
        local,
        mesh=mesh,
        in_specs=(
            P(None, None, "col", "row"),
            P(None, "row"),
            P(None, ("row", "col")),
            P(None, ("row", "col")),
            P(("row", "col"), None, None, None),
            P(None, "col", None),
        ),
        out_specs=(
            P(None, ("row", "col")),
            P(None, ("row", "col")),
            P(None, None, ("row", "col"), None),
        ),
        check_vma=False,
    )
```

```python
import math

import jax
import jax.numpy as jnp
from jax import lax
from jax.experimental import pallas as pl
from jax.experimental.pallas import tpu as pltpu
from jax.sharding import PartitionSpec as P

S = 256
BLK = 128
SLOTS = 6
PANEL = 16
SUB = 8
PITCH = S + 8
F32 = jnp.float32
BF16 = jnp.bfloat16
MESH = pl.DeviceIdType.MESH
VMEM_LIMIT = 56 << 20


def params():
    return pltpu.CompilerParams(vmem_limit_bytes=VMEM_LIMIT)


def split3(x):
    high = x.astype(BF16)
    rest = x - high.astype(F32)
    mid = rest.astype(BF16)
    low = (rest - mid.astype(F32)).astype(BF16)
    return high, mid, low


def dot3(a, b, dims):
    ah, am, _ = split3(a)
    bh, bm, _ = split3(b)
    dn = (dims, ((), ()))
    out = lax.dot_general(ah, bh, dn, preferred_element_type=F32)
    out += lax.dot_general(ah, bm, dn, preferred_element_type=F32)
    out += lax.dot_general(am, bh, dn, preferred_element_type=F32)
    return out


def terms_kernel(
    pattern_ref, map_ref, probe_ref, forward_ref, sparse_ref, child_ref,
    sent_ref, above_ref, own_ref, below_ref, blocked_ref,
    acc0, acc1, acc2, child, child_sem,
):
    b = pl.program_id(0)
    steps = pl.num_programs(0)
    row = lax.axis_index("row")
    accs = (acc0, acc1, acc2)
    fetch = pltpu.make_async_copy(child_ref, child, child_sem)

    @pl.when(b == 0)
    def _():
        fetch.start()
        for acc in accs:
            acc[...] = jnp.zeros_like(acc)

    blocked_ref[0] = forward_ref[...]
    probe = probe_ref[...]
    for s in range(0, SLOTS, 2):
        for q in range(3):
            slot = q * SLOTS + s
            pair = jnp.concatenate([sparse_ref[0, slot], sparse_ref[0, slot + 1]], axis=1)
            product = jnp.dot(probe, pair, preferred_element_type=F32)
            for i in range(2):
                target = pattern_ref[row, b, slot + i]
                accs[q][target] += product[:, i * BLK : (i + 1) * BLK]

    leaves = sent_ref.shape[0]
    blocks = sent_ref.shape[3] // BLK
    first_step = 4
    share = leaves // 4

    @pl.when(b == first_step)
    def _():
        fetch.wait()

    @pl.when(b >= first_step)
    def _():
        def leaf(i, carry):
            d = (b - first_step) * share + i
            for c in range(blocks):
                first = pl.multiple_of(map_ref[0, d * blocks + c] * BLK, BLK)
                second = pl.multiple_of(map_ref[1, d * blocks + c] * BLK, BLK)
                for k in range(2):
                    x = child[0, k, :, pl.ds(first, BLK)].astype(F32)
                    y = child[1, k, :, pl.ds(second, BLK)].astype(F32)
                    sent_ref[d, k, :, c * BLK : (c + 1) * BLK] = (x + y).astype(BF16)
            return carry

        lax.fori_loop(0, share, leaf, 0)

    @pl.when(b == steps - 1)
    def _():
        above_ref[...] = acc0[...].astype(BF16)
        own_ref[...] = acc1[...]
        below_ref[...] = acc2[...].astype(BF16)


def local_terms(pattern, child_map, probe, forward_probe, sparse, child_samples, leaves):
    blocks = sparse.shape[0]
    samples_here, rows_group = child_samples.shape[2:]
    shape = (blocks, S, BLK)
    sent = (leaves, 2, samples_here, rows_group // leaves)
    whole = pl.BlockSpec(shape, lambda b: (0, 0, 0))
    smem = pl.BlockSpec(memory_space=pltpu.SMEM)
    return pl.pallas_call(
        terms_kernel,
        grid=(blocks,),
        out_shape=[
            jax.ShapeDtypeStruct(sent, BF16),
            jax.ShapeDtypeStruct(shape, BF16),
            jax.ShapeDtypeStruct(shape, F32),
            jax.ShapeDtypeStruct(shape, BF16),
            jax.ShapeDtypeStruct(shape, BF16),
        ],
        in_specs=[
            smem,
            smem,
            pl.BlockSpec((S, BLK), lambda b: (0, b)),
            pl.BlockSpec((S, BLK), lambda b: (0, b)),
            pl.BlockSpec((1, 3 * SLOTS, BLK, BLK), lambda b: (b, 0, 0, 0)),
            pl.BlockSpec(memory_space=pl.ANY),
        ],
        out_specs=[pl.BlockSpec(sent, lambda b: (0, 0, 0, 0)), whole, whole, whole]
        + [pl.BlockSpec((1, S, BLK), lambda b: (b, 0, 0))],
        scratch_shapes=[pltpu.VMEM(shape, F32)] * 3
        + [pltpu.VMEM(child_samples.shape, BF16), pltpu.SemaphoreType.DMA],
        compiler_params=params(),
        name="terms",
    )(pattern, child_map, probe, forward_probe, sparse, child_samples)


def exchange_kernel(
    pattern_ref, probe_ref, sent_ref, above_ref, own_ref, below_ref, sparse_ref,
    samples_ref, gram_ref,
    ext, before, after, down, up, own, blocks, samples, gram, packed, partner,
    ext_send, ext_recv, row_send, row_recv, quad_send, quad_recv, local_sem, block_sem,
):
    row = lax.axis_index("row")
    col = lax.axis_index("col")
    n_row = lax.axis_size("row")
    n_col = lax.axis_size("col")
    n_blocks = blocks.shape[0]
    side = 4
    cx = col // side
    cy = col % side
    inner_up = row < n_row - 1
    inner_down = row > 0

    peers = []
    for d in range(1, n_col):
        px = (cx + d // side) % side
        py = (cy + d % side) % side
        peers.append(px * side + py)

    barrier = pltpu.get_barrier_semaphore()
    for peer in peers:
        pl.semaphore_signal(barrier, inc=1, device_id=(row, peer), device_id_type=MESH)

    for neighbour in ((row + 1) % n_row, (row + n_row - 1) % n_row):
        pl.semaphore_signal(barrier, inc=1, device_id=(neighbour, col), device_id_type=MESH)

    fetches = [
        pltpu.make_async_copy(sparse_ref.at[b], blocks.at[b], block_sem.at[b])
        for b in range(n_blocks)
    ]
    own_fetch = pltpu.make_async_copy(own_ref, own, local_sem.at[0])
    ext_fetch = pltpu.make_async_copy(sent_ref.at[col], ext.at[col], local_sem.at[1])
    for fetch in fetches:
        fetch.start()
    own_fetch.start()
    ext_fetch.start()

    @pl.when(row == 0)
    def _():
        before[...] = jnp.zeros_like(before)
        up[...] = jnp.zeros_like(up)

    @pl.when(row == n_row - 1)
    def _():
        after[...] = jnp.zeros_like(after)
        down[...] = jnp.zeros_like(down)

    def to_row(source, target, index, step):
        return pltpu.make_async_remote_copy(
            src_ref=source,
            dst_ref=target,
            send_sem=row_send.at[index],
            recv_sem=row_recv.at[index],
            device_id=(row + step, col),
            device_id_type=MESH,
        )

    rising = [to_row(probe_ref, before, 0, 1), to_row(below_ref, up, 1, 1)]
    falling = [to_row(probe_ref, after, 2, -1), to_row(above_ref, down, 3, -1)]

    pl.semaphore_wait(barrier, n_col + 1)

    @pl.when(inner_up)
    def _():
        rising[0].start()

    @pl.when(inner_down)
    def _():
        falling[0].start()

    spread = [
        pltpu.make_async_remote_copy(
            src_ref=sent_ref.at[peer],
            dst_ref=ext.at[col],
            send_sem=ext_send.at[i],
            recv_sem=ext_recv.at[i],
            device_id=(row, peer),
            device_id_type=MESH,
        )
        for i, peer in enumerate(peers)
    ]
    for copy in spread:
        copy.start()

    def product(b, regions):
        left = []
        right = []
        for q, source in regions:
            for s in range(q * SLOTS, (q + 1) * SLOTS):
                left.append(source[pattern_ref[row, b, s]])
                right.append(blocks[b, s])
        return lax.dot_general(
            jnp.concatenate(left, axis=1),
            jnp.concatenate(right, axis=1),
            (((1,), (1,)), ((), ())),
            preferred_element_type=F32,
        )

    for fetch in fetches:
        fetch.wait()

    def own_region(b, carry):
        lanes = pl.ds(pl.multiple_of(b * BLK, BLK), BLK)
        samples[0, :, lanes] = product(b, [(1, probe_ref)])
        return carry

    lax.fori_loop(0, n_blocks, own_region, 0)

    @pl.when(inner_down)
    def _():
        rising[0].wait_recv()

    @pl.when(inner_up)
    def _():
        falling[0].wait_recv()

    @pl.when(inner_up)
    def _():
        rising[1].start()

    @pl.when(inner_down)
    def _():
        falling[1].start()

    def other_regions(b, carry):
        lanes = pl.ds(pl.multiple_of(b * BLK, BLK), BLK)
        samples[0, :, lanes] += product(b, [(0, before), (2, after)])
        return carry

    lax.fori_loop(0, n_blocks, other_regions, 0)

    gram[...] = jnp.zeros_like(gram)
    row_id = lax.broadcasted_iota(jnp.int32, (BLK, BLK), 0)
    col_id = lax.broadcasted_iota(jnp.int32, (BLK, BLK), 1)
    quad = []

    def finish(k, other_terms):
        def assemble(h, carry):
            lanes = pl.ds(pl.multiple_of(h * 2 * BLK, 2 * BLK), 2 * BLK)
            y = ext[:, k, :, lanes].reshape(S, 2 * BLK).astype(F32) + other_terms(h, lanes)
            samples[k, :, lanes] = y
            gram[k] += dot3(y, y, ((1,), (1,)))
            return carry

        lax.fori_loop(0, n_blocks // 2, assemble, 0)
        last = gram[k, BLK:, BLK:]
        diagonal = jnp.sum(jnp.where(row_id == col_id, last, 0.0), axis=0, keepdims=True)
        pieces = (
            (0, gram[k, :BLK, BLK:]),
            (BLK, jnp.where(col_id >= row_id, gram[k, :BLK, :BLK], last)),
            (2 * BLK, jnp.broadcast_to(diagonal, (16, BLK))),
        )
        for at, piece in pieces:
            gram_ref[0, k, at : at + piece.shape[0]] = piece
            packed[k, at : at + piece.shape[0]] = piece.astype(BF16)
        copies = [
            pltpu.make_async_remote_copy(
                src_ref=packed.at[k],
                dst_ref=partner.at[i, k],
                send_sem=quad_send.at[3 * k + i],
                recv_sem=quad_recv.at[3 * k + i],
                device_id=(row, cx * side + other),
                device_id_type=MESH,
            )
            for i, other in enumerate((cy + 1 - 2 * (cy % 2), (cy + 2) % side, side - 1 - cy))
        ]
        for copy in copies:
            copy.start()
        quad.append(copies)

    ext_fetch.wait()
    for copy in spread:
        copy.wait_recv()
    finish(0, lambda h, lanes: samples[0, :, lanes])
    own_fetch.wait()

    @pl.when(inner_down)
    def _():
        rising[1].wait_recv()

    @pl.when(inner_up)
    def _():
        falling[1].wait_recv()

    def adjoint_terms(h, lanes):
        parts = []
        for c in range(2):
            at = h * 2 + c
            parts.append(own[at] + down[at].astype(F32) + up[at].astype(F32))
        return jnp.concatenate(parts, axis=1)

    finish(1, adjoint_terms)
    store = pltpu.make_async_copy(samples, samples_ref, local_sem.at[2])
    store.start()

    @pl.when(inner_up)
    def _():
        for copy in rising:
            copy.wait_send()

    @pl.when(inner_down)
    def _():
        for copy in falling:
            copy.wait_send()

    for copy in spread:
        copy.wait_send()
    for k in range(2):
        quad[k][0].wait_recv()
        gram_ref[1, k] = gram_ref[0, k] + partner[0, k].astype(F32)
        quad[k][1].wait_recv()
        quad[k][2].wait_recv()
        gram_ref[2, k] = gram_ref[1, k] + partner[1, k].astype(F32) + partner[2, k].astype(F32)
    for copies in quad:
        for copy in copies:
            copy.wait_send()
    store.wait()


def exchange(pattern, probe, sent, above, own, below, sparse):
    rows = sent.shape[3]
    leaves = sent.shape[0]
    held = 2 * BLK + 16
    anywhere = pl.BlockSpec(memory_space=pl.ANY)
    vmem = pl.BlockSpec(memory_space=pltpu.VMEM)
    dma = pltpu.SemaphoreType.DMA
    return pl.pallas_call(
        exchange_kernel,
        out_shape=[
            jax.ShapeDtypeStruct((2, S, rows), F32),
            jax.ShapeDtypeStruct((3, 2, held, BLK), F32),
        ],
        in_specs=[pl.BlockSpec(memory_space=pltpu.SMEM), vmem] + [anywhere] * 5,
        out_specs=[anywhere, vmem],
        scratch_shapes=[
            pltpu.VMEM(sent.shape, BF16),
            pltpu.VMEM(probe.shape, BF16),
            pltpu.VMEM(probe.shape, BF16),
            pltpu.VMEM(above.shape, BF16),
            pltpu.VMEM(below.shape, BF16),
            pltpu.VMEM(own.shape, F32),
            pltpu.VMEM(sparse.shape, BF16),
            pltpu.VMEM((2, S, rows), F32),
            pltpu.VMEM((2, S, S), F32),
            pltpu.VMEM((2, held, BLK), BF16),
            pltpu.VMEM((3, 2, held, BLK), BF16),
            dma((leaves - 1,)),
            dma((leaves - 1,)),
            dma((4,)),
            dma((4,)),
            dma((6,)),
            dma((6,)),
            dma((3,)),
            dma((sparse.shape[0],)),
        ],
        compiler_params=pltpu.CompilerParams(
            collective_id=0, has_side_effects=True, vmem_limit_bytes=VMEM_LIMIT
        ),
        name="exchange",
    )(pattern, probe, sent, above, own, below, sparse)


def splat(x, at):
    return jnp.broadcast_to(x[:, at:at+1], (8, BLK))

def eliminate(rows, first, half, lane):
    count=len(rows)
    for g in range(0, count, SUB):
        base=first+g
        e=[[splat(rows[g+j][half], base+i) if i>=j else None for i in range(SUB)] for j in range(SUB)]
        scale=[]; fac=[]
        for j in range(SUB):
            s=lax.rsqrt(e[j][j]); scale.append(s)
            f=[e[j][i]*s if i>j else None for i in range(SUB)]
            fac.append(f)
            for i in range(j+1,SUB):
                for l in range(i,SUB):
                    e[i][l]=e[i][l]-f[i]*f[l]
        clean=[]
        for j in range(SUB):
            here=lane==base+j
            z=[x*scale[j] for x in rows[g+j]]
            z[half]=jnp.where(here,scale[j],z[half])
            rows[g+j]=z
            for i in range(j+1,SUB):
                r=list(rows[g+i]); r[half]=jnp.where(here,0.0,r[half])
                rows[g+i]=[x-fac[j][i]*y for x,y in zip(r,z)]
            c=list(z); c[half]=jnp.where((lane>base+j)&(lane<base+SUB),0.0,z[half]); clean.append(c)
        for i in range(g+SUB,count):
            r=list(rows[i]); r[half]=jnp.where((lane>=base)&(lane<base+SUB),0.0,r[half])
            for j in range(SUB):
                z=clean[j]
                f=splat(z[half], first+i)
                r=[x-f*y for x,y in zip(r,z)]
            rows[i]=r
    return rows

def factorize(work, count):
    lane = lax.broadcasted_iota(jnp.int32, (8, BLK), 1)
    for lo in range(0, S, PANEL):
        half = lo // BLK
        rows = [
            [work[b][pl.ds(lo + i, 8, stride=PITCH), :] for b in range(2)] for i in range(PANEL)
        ]
        rows = eliminate(rows, lo - half*BLK, half, lane)
        for i in range(PANEL):
            for b in range(2):
                work[b][pl.ds(lo + i, 8, stride=PITCH), :] = rows[i][b]
        end = lo + PANEL
        if end == S:
            break
        row_id = lax.broadcasted_iota(jnp.int32, (PANEL, BLK), 0) + lo
        col_id = lax.broadcasted_iota(jnp.int32, (PANEL, BLK), 1) + BLK * half
        dead = (col_id > row_id) & (col_id < end)
        cols = lax.broadcasted_iota(jnp.int32, (S - end, BLK), 1) + BLK * half
        mine = (cols >= lo) & (cols < end)
        for m in range(count):
            base = m * PITCH
            panel = [work[b][base + lo : base + end, :] for b in range(2)]
            masked = [jnp.where(dead, 0.0, x) if b == half else x for b, x in enumerate(panel)]
            skip = end // BLK
            left = panel[1] if skip else jnp.concatenate(panel, axis=1)
            lh, lm, ll = split3(left)
            rh, rm, rl = split3(jnp.concatenate(masked, axis=1))
            product = lax.dot_general(
                jnp.concatenate([lh, lh, lm, lh, ll, lm], axis=0),
                jnp.concatenate([rh, rm, rh, rl, rh, rm], axis=0),
                (((0,), (0,)), ((), ())),
                preferred_element_type=F32,
            )[end - skip * BLK :]
            for b in range(2):
                old = work[b][base + end : base + S, :]
                if b == half:
                    old = jnp.where(mine, 0.0, old)
                work[b][base + end : base + S, :] = old - product[:, b * BLK : (b + 1) * BLK]


def load_grams(gram_ref, work):
    w0, w1 = work
    corner_row = lax.broadcasted_iota(jnp.int32, (BLK, BLK), 0)
    corner_col = lax.broadcasted_iota(jnp.int32, (BLK, BLK), 1)
    for m in range(8):
        held = gram_ref.at[m // 2 % 3, m % 2]
        shared = held[BLK : 2 * BLK]
        at = m * PITCH
        w0[at : at + BLK, :] = shared
        w1[at : at + BLK, :] = held[:BLK]
        w1[at + BLK : at + S, :] = jnp.where(
            corner_row == corner_col,
            jnp.broadcast_to(held[2 * BLK : 2 * BLK + 1], (BLK, BLK)),
            shared.T,
        )
        w0[at + BLK : at + S, :] = jnp.zeros((BLK, BLK), F32)


def factor_kernel(gram_ref, samples_ref, row_ref, col_ref, transfer_ref, w0, w1):
    work = (w0, w1)
    step = pl.program_id(0)
    width = row_ref.shape[1]

    @pl.when(step == 0)
    def _():
        load_grams(gram_ref, work)
        factorize(work, 6)

    row_id = lax.broadcasted_iota(jnp.int32, (S, S), 0)
    col_id = lax.broadcasted_iota(jnp.int32, (S, S), 1)
    gain = math.sqrt(2 * width)

    def read(level, k):
        at = (2 * level + k) * PITCH
        return jnp.concatenate([work[b][at : at + S, :] for b in range(2)], axis=1)

    def inverse(level, k):
        return jnp.where(col_id <= row_id, read(level, k), 0.0)

    def upper(level, k):
        x = read(level, k)
        return jnp.where(col_id > row_id, x, jnp.where(col_id == row_id, 1.0 / x, 0.0))

    for k in range(2):
        for part in range(2):

            @pl.when(step == 1 + 2 * k + part)
            def _():
                basis = dot3(inverse(0, k), samples_ref[0], ((1,), (0,))) * gain
                (row_ref, col_ref)[k][...] = basis.astype(BF16)
                transfer_ref[0, part] = dot3(upper(part, k), inverse(part + 1, k), ((1,), (1,)))


def later(step, start):
    return jnp.maximum(step - start, 0)


def factor(grams, samples):
    rows = samples.shape[2]
    return pl.pallas_call(
        factor_kernel,
        out_shape=[
            jax.ShapeDtypeStruct((S, rows), BF16),
            jax.ShapeDtypeStruct((S, rows), BF16),
            jax.ShapeDtypeStruct((2, 2, S, S), F32),
        ],
        grid=(5,),
        in_specs=[
            pl.BlockSpec(grams.shape, lambda i: (0, 0, 0, 0)),
            pl.BlockSpec((1, S, rows // 2), lambda i: (later(i, 1) // 2, 0, later(i, 1) % 2)),
        ],
        out_specs=[
            pl.BlockSpec((S, rows // 2), lambda i: (0, jnp.minimum(later(i, 1), 1))),
            pl.BlockSpec((S, rows // 2), lambda i: (0, jnp.minimum(later(i, 3), 1))),
            pl.BlockSpec((1, 2, S, S), lambda i: (later(i, 1) // 2, 0, 0, 0)),
        ],
        scratch_shapes=[pltpu.VMEM((8 * PITCH, BLK), F32)] * 2,
        compiler_params=params(),
        name="factor",
    )(grams, samples)


def local(
    child_samples, child_map, forward_probe, adjoint_probe, stored_sparse_blocks, block_pattern
):
    leaves = lax.axis_size("col")
    sent, above, own, below, blocked = local_terms(
        block_pattern, child_map, adjoint_probe, forward_probe, stored_sparse_blocks, child_samples, leaves
    )
    samples, grams = exchange(
        block_pattern, blocked, sent, above, own, below, stored_sparse_blocks
    )
    return tuple(factor(grams, samples))


def solution(mesh):
    return jax.shard_map(
        local,
        mesh=mesh,
        in_specs=(
            P(None, None, "col", "row"),
            P(None, "row"),
            P(None, ("row", "col")),
            P(None, ("row", "col")),
            P(("row", "col"), None, None, None),
            P(None, "col", None),
        ),
        out_specs=(
            P(None, ("row", "col")),
            P(None, ("row", "col")),
            P(None, None, ("row", "col"), None),
        ),
        check_vma=False,
    )
```

```python
import math

import jax
import jax.numpy as jnp
from jax import lax
from jax.experimental import pallas as pl
from jax.experimental.pallas import tpu as pltpu
from jax.sharding import PartitionSpec as P

S = 256
BLK = 128
SLOTS = 6
PANEL = 16
SUB = 8
PITCH = S + 8
F32 = jnp.float32
BF16 = jnp.bfloat16
MESH = pl.DeviceIdType.MESH
VMEM_LIMIT = 56 << 20


def params():
    return pltpu.CompilerParams(vmem_limit_bytes=VMEM_LIMIT)


def split3(x):
    high = x.astype(BF16)
    rest = x - high.astype(F32)
    mid = rest.astype(BF16)
    low = (rest - mid.astype(F32)).astype(BF16)
    return high, mid, low


def dot3(a, b, dims):
    ah, am, _ = split3(a)
    bh, bm, _ = split3(b)
    dn = (dims, ((), ()))
    out = lax.dot_general(ah, bh, dn, preferred_element_type=F32)
    out += lax.dot_general(ah, bm, dn, preferred_element_type=F32)
    out += lax.dot_general(am, bh, dn, preferred_element_type=F32)
    return out


def extend_kernel(
    map_ref, pattern_ref, child_ref, forward_ref, sent_ref, blocked_ref, prior_ref, final_ref
):
    row = lax.axis_index("row")
    leaves = sent_ref.shape[0]
    blocks = blocked_ref.shape[0]
    none = blocks * SLOTS
    for q in range(3):
        for c in range(blocks):
            final_ref[q, c] = none
    for b in range(blocks):
        blocked_ref[b] = forward_ref[:, b * BLK : (b + 1) * BLK]

    def link(b, s):
        q = s // SLOTS
        target = pattern_ref[row, b, s]
        prior_ref[b, s] = final_ref[q, target]
        final_ref[q, target] = b * SLOTS + s - q * SLOTS

    def leaf(d, carry):
        for c in range(blocks):
            first = pl.multiple_of(map_ref[0, d * blocks + c] * BLK, BLK)
            second = pl.multiple_of(map_ref[1, d * blocks + c] * BLK, BLK)
            for k in range(2):
                x = child_ref[0, k, :, pl.ds(first, BLK)].astype(F32)
                y = child_ref[1, k, :, pl.ds(second, BLK)].astype(F32)
                sent_ref[d, k, :, c * BLK : (c + 1) * BLK] = (x + y).astype(BF16)
        return carry

    def linked_leaf(d, carry):
        for s in range(3 * SLOTS):
            link(d, s)
        return leaf(d, carry)

    lax.fori_loop(0, blocks, linked_leaf, 0)
    lax.fori_loop(blocks, leaves, leaf, 0)


def extend(child_map, pattern, child_samples, forward_probe, leaves):
    samples_here, rows_group = child_samples.shape[2:]
    rows = forward_probe.shape[1]
    blocks = rows // BLK
    smem = pl.BlockSpec(memory_space=pltpu.SMEM)
    vmem = pl.BlockSpec(memory_space=pltpu.VMEM)
    return pl.pallas_call(
        extend_kernel,
        out_shape=[
            jax.ShapeDtypeStruct((leaves, 2, samples_here, rows_group // leaves), BF16),
            jax.ShapeDtypeStruct((blocks, S, BLK), BF16),
            jax.ShapeDtypeStruct((blocks, 3 * SLOTS), jnp.int32),
            jax.ShapeDtypeStruct((3, blocks), jnp.int32),
        ],
        in_specs=[smem, smem, vmem, vmem],
        out_specs=[vmem, vmem, smem, smem],
        compiler_params=params(),
        name="extend",
    )(child_map, pattern, child_samples, forward_probe)


def exchange_kernel(
    pattern_ref, prior_ref, final_ref, probe_ref, adjoint_ref, sent_ref, sparse_ref,
    samples_ref, gram_ref,
    ext, before, after, down, up, above, below, sums, blocks, samples, gram, packed, partner,
    ext_send, ext_recv, row_send, row_recv, quad_send, quad_recv, local_sem, block_sem,
):
    row = lax.axis_index("row")
    col = lax.axis_index("col")
    n_row = lax.axis_size("row")
    n_col = lax.axis_size("col")
    n_blocks = blocks.shape[0]
    side = 4
    cx = col // side
    cy = col % side
    inner_up = row < n_row - 1
    inner_down = row > 0

    peers = []
    for d in range(1, n_col):
        px = (cx + d // side) % side
        py = (cy + d % side) % side
        peers.append(px * side + py)

    barrier = pltpu.get_barrier_semaphore()
    for peer in peers:
        pl.semaphore_signal(barrier, inc=1, device_id=(row, peer), device_id_type=MESH)

    for neighbour in ((row + 1) % n_row, (row + n_row - 1) % n_row):
        pl.semaphore_signal(barrier, inc=1, device_id=(neighbour, col), device_id_type=MESH)

    fetches = [
        pltpu.make_async_copy(sparse_ref.at[b], blocks.at[b], block_sem.at[b])
        for b in range(n_blocks)
    ]
    ext_fetch = pltpu.make_async_copy(sent_ref.at[col], ext.at[col], local_sem.at[1])
    for fetch in fetches:
        fetch.start()
    ext_fetch.start()

    @pl.when(row == 0)
    def _():
        before[...] = jnp.zeros_like(before)
        up[...] = jnp.zeros_like(up)

    @pl.when(row == n_row - 1)
    def _():
        after[...] = jnp.zeros_like(after)
        down[...] = jnp.zeros_like(down)

    def to_row(source, target, index, step):
        return pltpu.make_async_remote_copy(
            src_ref=source,
            dst_ref=target,
            send_sem=row_send.at[index],
            recv_sem=row_recv.at[index],
            device_id=(row + step, col),
            device_id_type=MESH,
        )

    rising = [to_row(probe_ref, before, 0, 1), to_row(below, up, 1, 1)]
    falling = [to_row(probe_ref, after, 2, -1), to_row(above, down, 3, -1)]

    pl.semaphore_wait(barrier, n_col + 1)

    @pl.when(inner_up)
    def _():
        rising[0].start()

    @pl.when(inner_down)
    def _():
        falling[0].start()

    spread = [
        pltpu.make_async_remote_copy(
            src_ref=sent_ref.at[peer],
            dst_ref=ext.at[col],
            send_sem=ext_send.at[i],
            recv_sem=ext_recv.at[i],
            device_id=(row, peer),
            device_id_type=MESH,
        )
        for i, peer in enumerate(peers)
    ]
    for copy in spread:
        copy.start()

    def product(b, regions):
        left = []
        right = []
        for q, source in regions:
            for s in range(q * SLOTS, (q + 1) * SLOTS):
                left.append(source[pattern_ref[row, b, s]])
                right.append(blocks[b, s])
        return lax.dot_general(
            jnp.concatenate(left, axis=1),
            jnp.concatenate(right, axis=1),
            (((1,), (1,)), ((), ())),
            preferred_element_type=F32,
        )

    none = n_blocks * SLOTS
    for q in range(3):
        sums[q, none] = jnp.zeros((S, BLK), F32)
    for fetch in fetches:
        fetch.wait()

    def adjoint_regions(regions):
        def step(b, carry):
            probe = adjoint_ref[:, pl.ds(pl.multiple_of(b * BLK, BLK), BLK)]
            for s in range(0, SLOTS, 2):
                for q in regions:
                    slot = q * SLOTS + s
                    pair = jnp.concatenate([blocks[b, slot], blocks[b, slot + 1]], axis=1)
                    product = jnp.dot(probe, pair, preferred_element_type=F32)
                    for i in range(2):
                        sums[q, b * SLOTS + s + i] = (
                            product[:, i * BLK : (i + 1) * BLK]
                            + sums[q, prior_ref[b, slot + i]]
                        )
            return carry

        lax.fori_loop(0, n_blocks, step, 0)

    adjoint_regions((0, 2))

    def settle(c, carry):
        above[c] = sums[0, final_ref[0, c]].astype(BF16)
        below[c] = sums[2, final_ref[2, c]].astype(BF16)
        return carry

    lax.fori_loop(0, n_blocks, settle, 0)

    @pl.when(inner_up)
    def _():
        rising[1].start()

    @pl.when(inner_down)
    def _():
        falling[1].start()

    adjoint_regions((1,))

    def own_region(b, carry):
        lanes = pl.ds(pl.multiple_of(b * BLK, BLK), BLK)
        samples[0, :, lanes] = product(b, [(1, probe_ref)])
        return carry

    lax.fori_loop(0, n_blocks, own_region, 0)

    @pl.when(inner_down)
    def _():
        rising[0].wait_recv()

    @pl.when(inner_up)
    def _():
        falling[0].wait_recv()

    def other_regions(b, carry):
        lanes = pl.ds(pl.multiple_of(b * BLK, BLK), BLK)
        samples[0, :, lanes] += product(b, [(0, before), (2, after)])
        return carry

    lax.fori_loop(0, n_blocks, other_regions, 0)

    gram[...] = jnp.zeros_like(gram)
    row_id = lax.broadcasted_iota(jnp.int32, (BLK, BLK), 0)
    col_id = lax.broadcasted_iota(jnp.int32, (BLK, BLK), 1)
    quad = []

    def finish(k, other_terms):
        def assemble(h, carry):
            lanes = pl.ds(pl.multiple_of(h * 2 * BLK, 2 * BLK), 2 * BLK)
            y = ext[:, k, :, lanes].reshape(S, 2 * BLK).astype(F32) + other_terms(h, lanes)
            samples[k, :, lanes] = y
            gram[k] += dot3(y, y, ((1,), (1,)))
            return carry

        lax.fori_loop(0, n_blocks // 2, assemble, 0)
        last = gram[k, BLK:, BLK:]
        diagonal = jnp.sum(jnp.where(row_id == col_id, last, 0.0), axis=0, keepdims=True)
        pieces = (
            (0, gram[k, :BLK, BLK:]),
            (BLK, jnp.where(col_id >= row_id, gram[k, :BLK, :BLK], last)),
            (2 * BLK, jnp.broadcast_to(diagonal, (16, BLK))),
        )
        for at, piece in pieces:
            gram_ref[0, k, at : at + piece.shape[0]] = piece
            packed[k, at : at + piece.shape[0]] = piece.astype(BF16)
        copies = [
            pltpu.make_async_remote_copy(
                src_ref=packed.at[k],
                dst_ref=partner.at[i, k],
                send_sem=quad_send.at[3 * k + i],
                recv_sem=quad_recv.at[3 * k + i],
                device_id=(row, cx * side + other),
                device_id_type=MESH,
            )
            for i, other in enumerate((cy + 1 - 2 * (cy % 2), (cy + 2) % side, side - 1 - cy))
        ]
        for copy in copies:
            copy.start()
        quad.append(copies)

    ext_fetch.wait()
    for copy in spread:
        copy.wait_recv()
    finish(0, lambda h, lanes: samples[0, :, lanes])

    @pl.when(inner_down)
    def _():
        rising[1].wait_recv()

    @pl.when(inner_up)
    def _():
        falling[1].wait_recv()

    def adjoint_terms(h, lanes):
        parts = []
        for c in range(2):
            at = h * 2 + c
            parts.append(sums[1, final_ref[1, at]] + down[at].astype(F32) + up[at].astype(F32))
        return jnp.concatenate(parts, axis=1)

    finish(1, adjoint_terms)
    store = pltpu.make_async_copy(samples, samples_ref, local_sem.at[2])
    store.start()

    @pl.when(inner_up)
    def _():
        for copy in rising:
            copy.wait_send()

    @pl.when(inner_down)
    def _():
        for copy in falling:
            copy.wait_send()

    for copy in spread:
        copy.wait_send()
    for k in range(2):
        quad[k][0].wait_recv()
        gram_ref[1, k] = gram_ref[0, k] + partner[0, k].astype(F32)
        quad[k][1].wait_recv()
        quad[k][2].wait_recv()
        gram_ref[2, k] = gram_ref[1, k] + partner[1, k].astype(F32) + partner[2, k].astype(F32)
    for copies in quad:
        for copy in copies:
            copy.wait_send()
    store.wait()


def exchange(pattern, prior, final, probe, adjoint_probe, sent, sparse):
    rows = sent.shape[3]
    leaves = sent.shape[0]
    held = 2 * BLK + 16
    anywhere = pl.BlockSpec(memory_space=pl.ANY)
    vmem = pl.BlockSpec(memory_space=pltpu.VMEM)
    dma = pltpu.SemaphoreType.DMA
    return pl.pallas_call(
        exchange_kernel,
        out_shape=[
            jax.ShapeDtypeStruct((2, S, rows), F32),
            jax.ShapeDtypeStruct((3, 2, held, BLK), F32),
        ],
        in_specs=[pl.BlockSpec(memory_space=pltpu.SMEM)] * 3 + [vmem] * 2 + [anywhere] * 2,
        out_specs=[anywhere, vmem],
        scratch_shapes=[
            pltpu.VMEM(sent.shape, BF16),
            pltpu.VMEM(probe.shape, BF16),
            pltpu.VMEM(probe.shape, BF16),
            pltpu.VMEM(probe.shape, BF16),
            pltpu.VMEM(probe.shape, BF16),
            pltpu.VMEM(probe.shape, BF16),
            pltpu.VMEM(probe.shape, BF16),
            pltpu.VMEM((3, sparse.shape[0] * SLOTS + 1, S, BLK), F32),
            pltpu.VMEM(sparse.shape, BF16),
            pltpu.VMEM((2, S, rows), F32),
            pltpu.VMEM((2, S, S), F32),
            pltpu.VMEM((2, held, BLK), BF16),
            pltpu.VMEM((3, 2, held, BLK), BF16),
            dma((leaves - 1,)),
            dma((leaves - 1,)),
            dma((4,)),
            dma((4,)),
            dma((6,)),
            dma((6,)),
            dma((3,)),
            dma((sparse.shape[0],)),
        ],
        compiler_params=pltpu.CompilerParams(
            collective_id=0, has_side_effects=True, vmem_limit_bytes=VMEM_LIMIT
        ),
        name="exchange",
    )(pattern, prior, final, probe, adjoint_probe, sent, sparse)


def splat(x, at):
    return jnp.broadcast_to(x[:, at:at+1], (8, BLK))

def eliminate(rows, first, half, lane):
    count=len(rows)
    for g in range(0, count, SUB):
        base=first+g
        e=[[splat(rows[g+j][half], base+i) if i>=j else None for i in range(SUB)] for j in range(SUB)]
        scale=[]; fac=[]
        for j in range(SUB):
            s=lax.rsqrt(e[j][j]); scale.append(s)
            f=[e[j][i]*s if i>j else None for i in range(SUB)]
            fac.append(f)
            for i in range(j+1,SUB):
                for l in range(i,SUB):
                    e[i][l]=e[i][l]-f[i]*f[l]
        clean=[]
        for j in range(SUB):
            here=lane==base+j
            z=[x*scale[j] for x in rows[g+j]]
            z[half]=jnp.where(here,scale[j],z[half])
            rows[g+j]=z
            for i in range(j+1,SUB):
                r=list(rows[g+i]); r[half]=jnp.where(here,0.0,r[half])
                rows[g+i]=[x-fac[j][i]*y for x,y in zip(r,z)]
            c=list(z); c[half]=jnp.where((lane>base+j)&(lane<base+SUB),0.0,z[half]); clean.append(c)
        for i in range(g+SUB,count):
            r=list(rows[i]); r[half]=jnp.where((lane>=base)&(lane<base+SUB),0.0,r[half])
            for j in range(SUB):
                z=clean[j]
                f=splat(z[half], first+i)
                r=[x-f*y for x,y in zip(r,z)]
            rows[i]=r
    return rows

def factorize(work, count):
    lane = lax.broadcasted_iota(jnp.int32, (8, BLK), 1)
    for lo in range(0, S, PANEL):
        half = lo // BLK
        rows = [
            [work[b][pl.ds(lo + i, 8, stride=PITCH), :] for b in range(2)] for i in range(PANEL)
        ]
        rows = eliminate(rows, lo - half*BLK, half, lane)
        for i in range(PANEL):
            for b in range(2):
                work[b][pl.ds(lo + i, 8, stride=PITCH), :] = rows[i][b]
        end = lo + PANEL
        if end == S:
            break
        row_id = lax.broadcasted_iota(jnp.int32, (PANEL, BLK), 0) + lo
        col_id = lax.broadcasted_iota(jnp.int32, (PANEL, BLK), 1) + BLK * half
        dead = (col_id > row_id) & (col_id < end)
        cols = lax.broadcasted_iota(jnp.int32, (S - end, BLK), 1) + BLK * half
        mine = (cols >= lo) & (cols < end)
        for m in range(count):
            base = m * PITCH
            panel = [work[b][base + lo : base + end, :] for b in range(2)]
            masked = [jnp.where(dead, 0.0, x) if b == half else x for b, x in enumerate(panel)]
            skip = end // BLK
            left = panel[1] if skip else jnp.concatenate(panel, axis=1)
            lh, lm, ll = split3(left)
            rh, rm, rl = split3(jnp.concatenate(masked, axis=1))
            product = lax.dot_general(
                jnp.concatenate([lh, lh, lm, lh, ll, lm], axis=0),
                jnp.concatenate([rh, rm, rh, rl, rh, rm], axis=0),
                (((0,), (0,)), ((), ())),
                preferred_element_type=F32,
            )[end - skip * BLK :]
            for b in range(2):
                old = work[b][base + end : base + S, :]
                if b == half:
                    old = jnp.where(mine, 0.0, old)
                work[b][base + end : base + S, :] = old - product[:, b * BLK : (b + 1) * BLK]


def load_grams(gram_ref, work):
    w0, w1 = work
    corner_row = lax.broadcasted_iota(jnp.int32, (BLK, BLK), 0)
    corner_col = lax.broadcasted_iota(jnp.int32, (BLK, BLK), 1)
    for m in range(8):
        held = gram_ref.at[m // 2 % 3, m % 2]
        shared = held[BLK : 2 * BLK]
        at = m * PITCH
        w0[at : at + BLK, :] = shared
        w1[at : at + BLK, :] = held[:BLK]
        w1[at + BLK : at + S, :] = jnp.where(
            corner_row == corner_col,
            jnp.broadcast_to(held[2 * BLK : 2 * BLK + 1], (BLK, BLK)),
            shared.T,
        )
        w0[at + BLK : at + S, :] = jnp.zeros((BLK, BLK), F32)


def factor_kernel(gram_ref, samples_ref, row_ref, col_ref, transfer_ref, w0, w1):
    work = (w0, w1)
    load_grams(gram_ref, work)
    factorize(work, 6)
    row_id = lax.broadcasted_iota(jnp.int32, (S, S), 0)
    col_id = lax.broadcasted_iota(jnp.int32, (S, S), 1)
    gain = math.sqrt(samples_ref.shape[2])
    for k in range(2):
        found = []
        for level in range(3):
            at = (2 * level + k) * PITCH
            found.append(jnp.concatenate([work[b][at : at + S, :] for b in range(2)], axis=1))
        inverse = [jnp.where(col_id <= row_id, x, 0.0) for x in found]
        upper = [
            jnp.where(col_id > row_id, x, jnp.where(col_id == row_id, 1.0 / x, 0.0))
            for x in found[:2]
        ]
        basis = dot3(inverse[0], samples_ref[k], ((1,), (0,))) * gain
        (row_ref, col_ref)[k][...] = basis.astype(BF16)
        for level in range(2):
            transfer_ref[k, level] = dot3(upper[level], inverse[level + 1], ((1,), (1,)))


def factor(grams, samples):
    rows = samples.shape[2]
    vmem = pl.BlockSpec(memory_space=pltpu.VMEM)
    return pl.pallas_call(
        factor_kernel,
        out_shape=[
            jax.ShapeDtypeStruct((S, rows), BF16),
            jax.ShapeDtypeStruct((S, rows), BF16),
            jax.ShapeDtypeStruct((2, 2, S, S), F32),
        ],
        in_specs=[vmem] * 2,
        out_specs=[vmem] * 3,
        scratch_shapes=[pltpu.VMEM((8 * PITCH, BLK), F32)] * 2,
        compiler_params=params(),
        name="factor",
    )(grams, samples)


def local(
    child_samples, child_map, forward_probe, adjoint_probe, stored_sparse_blocks, block_pattern
):
    leaves = lax.axis_size("col")
    sent, blocked, prior, final = extend(
        child_map, block_pattern, child_samples, forward_probe, leaves
    )
    samples, grams = exchange(
        block_pattern, prior, final, blocked, adjoint_probe, sent, stored_sparse_blocks
    )
    return tuple(factor(grams, samples))


def solution(mesh):
    return jax.shard_map(
        local,
        mesh=mesh,
        in_specs=(
            P(None, None, "col", "row"),
            P(None, "row"),
            P(None, ("row", "col")),
            P(None, ("row", "col")),
            P(("row", "col"), None, None, None),
            P(None, "col", None),
        ),
        out_specs=(
            P(None, ("row", "col")),
            P(None, ("row", "col")),
            P(None, None, ("row", "col"), None),
        ),
        check_vma=False,
    )
```

```python
import math

import jax
import jax.numpy as jnp
from jax import lax
from jax.experimental import pallas as pl
from jax.experimental.pallas import tpu as pltpu
from jax.sharding import PartitionSpec as P

S = 256
BLK = 128
SLOTS = 6
PANEL = 16
SUB = 8
PITCH = S + 8
F32 = jnp.float32
BF16 = jnp.bfloat16
MESH = pl.DeviceIdType.MESH
VMEM_LIMIT = 56 << 20


def params():
    return pltpu.CompilerParams(vmem_limit_bytes=VMEM_LIMIT)


def split3(x):
    high = x.astype(BF16)
    rest = x - high.astype(F32)
    mid = rest.astype(BF16)
    low = (rest - mid.astype(F32)).astype(BF16)
    return high, mid, low


def dot3(a, b, dims):
    ah, am, _ = split3(a)
    bh, bm, _ = split3(b)
    dn = (dims, ((), ()))
    out = lax.dot_general(ah, bh, dn, preferred_element_type=F32)
    out += lax.dot_general(ah, bm, dn, preferred_element_type=F32)
    out += lax.dot_general(am, bh, dn, preferred_element_type=F32)
    return out


def extend_kernel(
    map_ref, pattern_ref, child_ref, forward_ref, sent_ref, blocked_ref, prior_ref, final_ref
):
    row = lax.axis_index("row")
    leaves = sent_ref.shape[0]
    blocks = blocked_ref.shape[0]
    none = blocks * SLOTS
    for q in range(3):
        for c in range(blocks):
            final_ref[q, c] = none
    for b in range(blocks):
        blocked_ref[b] = forward_ref[:, b * BLK : (b + 1) * BLK]

    def link(b, s):
        q = s // SLOTS
        target = pattern_ref[row, b, s]
        prior_ref[b, s] = final_ref[q, target]
        final_ref[q, target] = b * SLOTS + s - q * SLOTS

    def leaf(d, carry):
        for c in range(blocks):
            first = pl.multiple_of(map_ref[0, d * blocks + c] * BLK, BLK)
            second = pl.multiple_of(map_ref[1, d * blocks + c] * BLK, BLK)
            for k in range(2):
                x = child_ref[0, k, :, pl.ds(first, BLK)].astype(F32)
                y = child_ref[1, k, :, pl.ds(second, BLK)].astype(F32)
                sent_ref[d, k, :, c * BLK : (c + 1) * BLK] = (x + y).astype(BF16)
        return carry

    def linked_leaf(d, carry):
        for s in range(3 * SLOTS):
            link(d, s)
        return leaf(d, carry)

    lax.fori_loop(0, blocks, linked_leaf, 0)
    lax.fori_loop(blocks, leaves, leaf, 0)


def extend(child_map, pattern, child_samples, forward_probe, leaves):
    samples_here, rows_group = child_samples.shape[2:]
    rows = forward_probe.shape[1]
    blocks = rows // BLK
    smem = pl.BlockSpec(memory_space=pltpu.SMEM)
    vmem = pl.BlockSpec(memory_space=pltpu.VMEM)
    return pl.pallas_call(
        extend_kernel,
        out_shape=[
            jax.ShapeDtypeStruct((leaves, 2, samples_here, rows_group // leaves), BF16),
            jax.ShapeDtypeStruct((blocks, S, BLK), BF16),
            jax.ShapeDtypeStruct((blocks, 3 * SLOTS), jnp.int32),
            jax.ShapeDtypeStruct((3, blocks), jnp.int32),
        ],
        in_specs=[smem, smem, vmem, vmem],
        out_specs=[vmem, vmem, smem, smem],
        compiler_params=params(),
        name="extend",
    )(child_map, pattern, child_samples, forward_probe)


def exchange_kernel(
    pattern_ref, prior_ref, final_ref, probe_ref, adjoint_ref, sent_ref, sparse_ref,
    samples_ref, gram_ref,
    ext, before, after, down, up, above, below, sums, blocks, samples, gram, packed, partner,
    ext_send, ext_recv, row_send, row_recv, quad_send, quad_recv, local_sem, block_sem,
):
    row = lax.axis_index("row")
    col = lax.axis_index("col")
    n_row = lax.axis_size("row")
    n_col = lax.axis_size("col")
    n_blocks = blocks.shape[0]
    side = 4
    cx = col // side
    cy = col % side
    inner_up = row < n_row - 1
    inner_down = row > 0

    peers = []
    for d in range(1, n_col):
        px = (cx + d // side) % side
        py = (cy + d % side) % side
        peers.append(px * side + py)

    barrier = pltpu.get_barrier_semaphore()
    for peer in peers:
        pl.semaphore_signal(barrier, inc=1, device_id=(row, peer), device_id_type=MESH)

    for neighbour in ((row + 1) % n_row, (row + n_row - 1) % n_row):
        pl.semaphore_signal(barrier, inc=1, device_id=(neighbour, col), device_id_type=MESH)

    fetches = [
        pltpu.make_async_copy(sparse_ref.at[b], blocks.at[b], block_sem.at[b])
        for b in range(n_blocks)
    ]
    ext_fetch = pltpu.make_async_copy(sent_ref.at[col], ext.at[col], local_sem.at[1])
    for fetch in fetches:
        fetch.start()
    ext_fetch.start()

    @pl.when(row == 0)
    def _():
        before[...] = jnp.zeros_like(before)
        up[...] = jnp.zeros_like(up)

    @pl.when(row == n_row - 1)
    def _():
        after[...] = jnp.zeros_like(after)
        down[...] = jnp.zeros_like(down)

    def to_row(source, target, index, step):
        return pltpu.make_async_remote_copy(
            src_ref=source,
            dst_ref=target,
            send_sem=row_send.at[index],
            recv_sem=row_recv.at[index],
            device_id=(row + step, col),
            device_id_type=MESH,
        )

    rising = [to_row(probe_ref, before, 0, 1), to_row(below, up, 1, 1)]
    falling = [to_row(probe_ref, after, 2, -1), to_row(above, down, 3, -1)]

    none = n_blocks * SLOTS
    for q in range(3):
        sums[q, none] = jnp.zeros((S, BLK), F32)
    def adjoint_regions(regions, begin, end):
        def step(b, carry):
            probe = adjoint_ref[:, pl.ds(pl.multiple_of(b * BLK, BLK), BLK)]
            for s in range(0, SLOTS, 2):
                for q in regions:
                    slot = q * SLOTS + s
                    pair = jnp.concatenate([blocks[b, slot], blocks[b, slot + 1]], axis=1)
                    product = jnp.dot(probe, pair, preferred_element_type=F32)
                    for i in range(2):
                        sums[q, b * SLOTS + s + i] = (
                            product[:, i * BLK : (i + 1) * BLK]
                            + sums[q, prior_ref[b, slot + i]]
                        )
            return carry

        lax.fori_loop(begin, end, step, 0)

    early = n_blocks // 2
    for fetch in fetches[:early]:
        fetch.wait()
    adjoint_regions((0, 2), 0, early)
    pl.semaphore_wait(barrier, n_col + 1)

    @pl.when(inner_up)
    def _():
        rising[0].start()

    @pl.when(inner_down)
    def _():
        falling[0].start()

    spread = [
        pltpu.make_async_remote_copy(
            src_ref=sent_ref.at[peer, k],
            dst_ref=ext.at[col, k],
            send_sem=ext_send.at[k, i],
            recv_sem=ext_recv.at[k, i],
            device_id=(row, peer),
            device_id_type=MESH,
        )
        for k in range(2)
        for i, peer in enumerate(peers)
    ]
    for copy in spread:
        copy.start()

    def product(b, regions):
        left = []
        right = []
        for q, source in regions:
            for s in range(q * SLOTS, (q + 1) * SLOTS):
                left.append(source[pattern_ref[row, b, s]])
                right.append(blocks[b, s])
        return lax.dot_general(
            jnp.concatenate(left, axis=1),
            jnp.concatenate(right, axis=1),
            (((1,), (1,)), ((), ())),
            preferred_element_type=F32,
        )

    for fetch in fetches[early:]:
        fetch.wait()
    adjoint_regions((0, 2), early, n_blocks)

    def settle(c, carry):
        above[c] = sums[0, final_ref[0, c]].astype(BF16)
        below[c] = sums[2, final_ref[2, c]].astype(BF16)
        return carry

    lax.fori_loop(0, n_blocks, settle, 0)

    @pl.when(inner_up)
    def _():
        rising[1].start()

    @pl.when(inner_down)
    def _():
        falling[1].start()

    def own_region(b, carry):
        lanes = pl.ds(pl.multiple_of(b * BLK, BLK), BLK)
        samples[0, :, lanes] = product(b, [(1, probe_ref)])
        return carry

    lax.fori_loop(0, n_blocks, own_region, 0)

    @pl.when(inner_down)
    def _():
        rising[0].wait_recv()

    @pl.when(inner_up)
    def _():
        falling[0].wait_recv()

    def other_regions(b, carry):
        lanes = pl.ds(pl.multiple_of(b * BLK, BLK), BLK)
        samples[0, :, lanes] += product(b, [(0, before), (2, after)])
        return carry

    lax.fori_loop(0, n_blocks, other_regions, 0)

    gram[...] = jnp.zeros_like(gram)
    row_id = lax.broadcasted_iota(jnp.int32, (BLK, BLK), 0)
    col_id = lax.broadcasted_iota(jnp.int32, (BLK, BLK), 1)
    quad = []

    def finish(k, other_terms):
        def assemble(h, carry):
            lanes = pl.ds(pl.multiple_of(h * 2 * BLK, 2 * BLK), 2 * BLK)
            y = ext[:, k, :, lanes].reshape(S, 2 * BLK).astype(F32) + other_terms(h, lanes)
            samples[k, :, lanes] = y
            gram[k] += dot3(y, y, ((1,), (1,)))
            return carry

        lax.fori_loop(0, n_blocks // 2, assemble, 0)
        last = gram[k, BLK:, BLK:]
        diagonal = jnp.sum(jnp.where(row_id == col_id, last, 0.0), axis=0, keepdims=True)
        pieces = (
            (0, gram[k, :BLK, BLK:]),
            (BLK, jnp.where(col_id >= row_id, gram[k, :BLK, :BLK], last)),
            (2 * BLK, jnp.broadcast_to(diagonal, (16, BLK))),
        )
        for at, piece in pieces:
            gram_ref[0, k, at : at + piece.shape[0]] = piece
            packed[k, at : at + piece.shape[0]] = piece.astype(BF16)
        copies = [
            pltpu.make_async_remote_copy(
                src_ref=packed.at[k],
                dst_ref=partner.at[i, k],
                send_sem=quad_send.at[3 * k + i],
                recv_sem=quad_recv.at[3 * k + i],
                device_id=(row, cx * side + other),
                device_id_type=MESH,
            )
            for i, other in enumerate((cy + 1 - 2 * (cy % 2), (cy + 2) % side, side - 1 - cy))
        ]
        for copy in copies:
            copy.start()
        quad.append(copies)

    ext_fetch.wait()
    for copy in spread[: n_col - 1]:
        copy.wait_recv()
    finish(0, lambda h, lanes: samples[0, :, lanes])
    adjoint_regions((1,), 0, n_blocks)
    for copy in spread[n_col - 1 :]:
        copy.wait_recv()

    @pl.when(inner_down)
    def _():
        rising[1].wait_recv()

    @pl.when(inner_up)
    def _():
        falling[1].wait_recv()

    def adjoint_terms(h, lanes):
        parts = []
        for c in range(2):
            at = h * 2 + c
            parts.append(sums[1, final_ref[1, at]] + down[at].astype(F32) + up[at].astype(F32))
        return jnp.concatenate(parts, axis=1)

    finish(1, adjoint_terms)
    store = pltpu.make_async_copy(samples, samples_ref, local_sem.at[2])
    store.start()

    @pl.when(inner_up)
    def _():
        for copy in rising:
            copy.wait_send()

    @pl.when(inner_down)
    def _():
        for copy in falling:
            copy.wait_send()

    for copy in spread:
        copy.wait_send()
    for k in range(2):
        quad[k][0].wait_recv()
        gram_ref[1, k] = gram_ref[0, k] + partner[0, k].astype(F32)
        quad[k][1].wait_recv()
        quad[k][2].wait_recv()
        gram_ref[2, k] = gram_ref[1, k] + partner[1, k].astype(F32) + partner[2, k].astype(F32)
    for copies in quad:
        for copy in copies:
            copy.wait_send()
    store.wait()


def exchange(pattern, prior, final, probe, adjoint_probe, sent, sparse):
    rows = sent.shape[3]
    leaves = sent.shape[0]
    held = 2 * BLK + 16
    anywhere = pl.BlockSpec(memory_space=pl.ANY)
    vmem = pl.BlockSpec(memory_space=pltpu.VMEM)
    dma = pltpu.SemaphoreType.DMA
    return pl.pallas_call(
        exchange_kernel,
        out_shape=[
            jax.ShapeDtypeStruct((2, S, rows), F32),
            jax.ShapeDtypeStruct((3, 2, held, BLK), F32),
        ],
        in_specs=[pl.BlockSpec(memory_space=pltpu.SMEM)] * 3 + [vmem] * 2 + [anywhere] * 2,
        out_specs=[anywhere, vmem],
        scratch_shapes=[
            pltpu.VMEM(sent.shape, BF16),
            pltpu.VMEM(probe.shape, BF16),
            pltpu.VMEM(probe.shape, BF16),
            pltpu.VMEM(probe.shape, BF16),
            pltpu.VMEM(probe.shape, BF16),
            pltpu.VMEM(probe.shape, BF16),
            pltpu.VMEM(probe.shape, BF16),
            pltpu.VMEM((3, sparse.shape[0] * SLOTS + 1, S, BLK), F32),
            pltpu.VMEM(sparse.shape, BF16),
            pltpu.VMEM((2, S, rows), F32),
            pltpu.VMEM((2, S, S), F32),
            pltpu.VMEM((2, held, BLK), BF16),
            pltpu.VMEM((3, 2, held, BLK), BF16),
            dma((2, leaves - 1)),
            dma((2, leaves - 1)),
            dma((4,)),
            dma((4,)),
            dma((6,)),
            dma((6,)),
            dma((3,)),
            dma((sparse.shape[0],)),
        ],
        compiler_params=pltpu.CompilerParams(
            collective_id=0, has_side_effects=True, vmem_limit_bytes=VMEM_LIMIT
        ),
        name="exchange",
    )(pattern, prior, final, probe, adjoint_probe, sent, sparse)


def splat(x, at):
    return jnp.broadcast_to(x[:, at:at+1], (8, BLK))

def eliminate(rows, first, half, lane):
    count=len(rows)
    for g in range(0, count, SUB):
        base=first+g
        e=[[splat(rows[g+j][half], base+i) if i>=j else None for i in range(SUB)] for j in range(SUB)]
        scale=[]; fac=[]
        for j in range(SUB):
            s=lax.rsqrt(e[j][j]); scale.append(s)
            f=[e[j][i]*s if i>j else None for i in range(SUB)]
            fac.append(f)
            for i in range(j+1,SUB):
                for l in range(i,SUB):
                    e[i][l]=e[i][l]-f[i]*f[l]
        clean=[]
        for j in range(SUB):
            here=lane==base+j
            z=[x*scale[j] for x in rows[g+j]]
            z[half]=jnp.where(here,scale[j],z[half])
            rows[g+j]=z
            for i in range(j+1,SUB):
                r=list(rows[g+i]); r[half]=jnp.where(here,0.0,r[half])
                rows[g+i]=[x-fac[j][i]*y for x,y in zip(r,z)]
            c=list(z); c[half]=jnp.where((lane>base+j)&(lane<base+SUB),0.0,z[half]); clean.append(c)
        for i in range(g+SUB,count):
            r=list(rows[i]); r[half]=jnp.where((lane>=base)&(lane<base+SUB),0.0,r[half])
            for j in range(SUB):
                z=clean[j]
                f=splat(z[half], first+i)
                r=[x-f*y for x,y in zip(r,z)]
            rows[i]=r
    return rows

def factorize(work, count):
    lane = lax.broadcasted_iota(jnp.int32, (8, BLK), 1)
    for lo in range(0, S, PANEL):
        half = lo // BLK
        rows = [
            [work[b][pl.ds(lo + i, 8, stride=PITCH), :] for b in range(2)] for i in range(PANEL)
        ]
        rows = eliminate(rows, lo - half*BLK, half, lane)
        for i in range(PANEL):
            for b in range(2):
                work[b][pl.ds(lo + i, 8, stride=PITCH), :] = rows[i][b]
        end = lo + PANEL
        if end == S:
            break
        row_id = lax.broadcasted_iota(jnp.int32, (PANEL, BLK), 0) + lo
        col_id = lax.broadcasted_iota(jnp.int32, (PANEL, BLK), 1) + BLK * half
        dead = (col_id > row_id) & (col_id < end)
        cols = lax.broadcasted_iota(jnp.int32, (S - end, BLK), 1) + BLK * half
        mine = (cols >= lo) & (cols < end)
        for m in range(count):
            base = m * PITCH
            panel = [work[b][base + lo : base + end, :] for b in range(2)]
            masked = [jnp.where(dead, 0.0, x) if b == half else x for b, x in enumerate(panel)]
            skip = end // BLK
            left = panel[1] if skip else jnp.concatenate(panel, axis=1)
            lh, lm, ll = split3(left)
            rh, rm, rl = split3(jnp.concatenate(masked, axis=1))
            product = lax.dot_general(
                jnp.concatenate([lh, lh, lm, lh, ll, lm], axis=0),
                jnp.concatenate([rh, rm, rh, rl, rh, rm], axis=0),
                (((0,), (0,)), ((), ())),
                preferred_element_type=F32,
            )[end - skip * BLK :]
            for b in range(2):
                old = work[b][base + end : base + S, :]
                if b == half:
                    old = jnp.where(mine, 0.0, old)
                work[b][base + end : base + S, :] = old - product[:, b * BLK : (b + 1) * BLK]


def load_grams(gram_ref, work):
    w0, w1 = work
    corner_row = lax.broadcasted_iota(jnp.int32, (BLK, BLK), 0)
    corner_col = lax.broadcasted_iota(jnp.int32, (BLK, BLK), 1)
    for m in range(8):
        held = gram_ref.at[m // 2 % 3, m % 2]
        shared = held[BLK : 2 * BLK]
        at = m * PITCH
        w0[at : at + BLK, :] = shared
        w1[at : at + BLK, :] = held[:BLK]
        w1[at + BLK : at + S, :] = jnp.where(
            corner_row == corner_col,
            jnp.broadcast_to(held[2 * BLK : 2 * BLK + 1], (BLK, BLK)),
            shared.T,
        )
        w0[at + BLK : at + S, :] = jnp.zeros((BLK, BLK), F32)


def factor_kernel(gram_ref, samples_ref, row_ref, col_ref, transfer_ref, w0, w1):
    work = (w0, w1)
    load_grams(gram_ref, work)
    factorize(work, 6)
    row_id = lax.broadcasted_iota(jnp.int32, (S, S), 0)
    col_id = lax.broadcasted_iota(jnp.int32, (S, S), 1)
    gain = math.sqrt(samples_ref.shape[2])
    for k in range(2):
        found = []
        for level in range(3):
            at = (2 * level + k) * PITCH
            found.append(jnp.concatenate([work[b][at : at + S, :] for b in range(2)], axis=1))
        inverse = [jnp.where(col_id <= row_id, x, 0.0) for x in found]
        upper = [
            jnp.where(col_id > row_id, x, jnp.where(col_id == row_id, 1.0 / x, 0.0))
            for x in found[:2]
        ]
        basis = dot3(inverse[0], samples_ref[k], ((1,), (0,))) * gain
        (row_ref, col_ref)[k][...] = basis.astype(BF16)
        for level in range(2):
            transfer_ref[k, level] = dot3(upper[level], inverse[level + 1], ((1,), (1,)))


def factor(grams, samples):
    rows = samples.shape[2]
    vmem = pl.BlockSpec(memory_space=pltpu.VMEM)
    return pl.pallas_call(
        factor_kernel,
        out_shape=[
            jax.ShapeDtypeStruct((S, rows), BF16),
            jax.ShapeDtypeStruct((S, rows), BF16),
            jax.ShapeDtypeStruct((2, 2, S, S), F32),
        ],
        in_specs=[vmem] * 2,
        out_specs=[vmem] * 3,
        scratch_shapes=[pltpu.VMEM((8 * PITCH, BLK), F32)] * 2,
        compiler_params=params(),
        name="factor",
    )(grams, samples)


def local(
    child_samples, child_map, forward_probe, adjoint_probe, stored_sparse_blocks, block_pattern
):
    leaves = lax.axis_size("col")
    sent, blocked, prior, final = extend(
        child_map, block_pattern, child_samples, forward_probe, leaves
    )
    samples, grams = exchange(
        block_pattern, prior, final, blocked, adjoint_probe, sent, stored_sparse_blocks
    )
    return tuple(factor(grams, samples))


def solution(mesh):
    return jax.shard_map(
        local,
        mesh=mesh,
        in_specs=(
            P(None, None, "col", "row"),
            P(None, "row"),
            P(None, ("row", "col")),
            P(None, ("row", "col")),
            P(("row", "col"), None, None, None),
            P(None, "col", None),
        ),
        out_specs=(
            P(None, ("row", "col")),
            P(None, ("row", "col")),
            P(None, None, ("row", "col"), None),
        ),
        check_vma=False,
    )
```

```python
from functools import partial
import math

import jax
import jax.numpy as jnp
from jax import lax
from jax.experimental import pallas as pl
from jax.experimental.pallas import tpu as pltpu
from jax.sharding import PartitionSpec as P

S = 256
BLK = 128
SLOTS = 6
PANEL = 16
SUB = 8
PITCH = S + 8
F32 = jnp.float32
BF16 = jnp.bfloat16
MESH = pl.DeviceIdType.MESH
VMEM_LIMIT = 56 << 20


def params():
    return pltpu.CompilerParams(vmem_limit_bytes=VMEM_LIMIT)


def split3(x):
    high = x.astype(BF16)
    rest = x - high.astype(F32)
    mid = rest.astype(BF16)
    low = (rest - mid.astype(F32)).astype(BF16)
    return high, mid, low


def dot3(a, b, dims):
    ah, am, _ = split3(a)
    bh, bm, _ = split3(b)
    dn = (dims, ((), ()))
    out = lax.dot_general(ah, bh, dn, preferred_element_type=F32)
    out += lax.dot_general(ah, bm, dn, preferred_element_type=F32)
    out += lax.dot_general(am, bh, dn, preferred_element_type=F32)
    return out


def extend_kernel(
    map_ref, pattern_ref, child_ref, forward_ref, sent_ref, blocked_ref, prior_ref, final_ref
):
    row = lax.axis_index("row")
    leaves = sent_ref.shape[0]
    blocks = blocked_ref.shape[0]
    none = blocks * SLOTS
    for q in range(3):
        for c in range(blocks):
            final_ref[q, c] = none
    for b in range(blocks):
        blocked_ref[b] = forward_ref[:, b * BLK : (b + 1) * BLK]

    def link(b, s):
        q = s // SLOTS
        target = pattern_ref[row, b, s]
        prior_ref[b, s] = final_ref[q, target]
        final_ref[q, target] = b * SLOTS + s - q * SLOTS

    def leaf(d, carry):
        for c in range(blocks):
            first = pl.multiple_of(map_ref[0, d * blocks + c] * BLK, BLK)
            second = pl.multiple_of(map_ref[1, d * blocks + c] * BLK, BLK)
            for k in range(2):
                x = child_ref[0, k, :, pl.ds(first, BLK)].astype(F32)
                y = child_ref[1, k, :, pl.ds(second, BLK)].astype(F32)
                sent_ref[d, k, :, c * BLK : (c + 1) * BLK] = (x + y).astype(BF16)
        return carry

    def linked_leaf(d, carry):
        for s in range(3 * SLOTS):
            link(d, s)
        return leaf(d, carry)

    lax.fori_loop(0, blocks, linked_leaf, 0)
    lax.fori_loop(blocks, leaves, leaf, 0)


def extend(child_map, pattern, child_samples, forward_probe, leaves):
    samples_here, rows_group = child_samples.shape[2:]
    rows = forward_probe.shape[1]
    blocks = rows // BLK
    smem = pl.BlockSpec(memory_space=pltpu.SMEM)
    vmem = pl.BlockSpec(memory_space=pltpu.VMEM)
    return pl.pallas_call(
        extend_kernel,
        out_shape=[
            jax.ShapeDtypeStruct((leaves, 2, samples_here, rows_group // leaves), BF16),
            jax.ShapeDtypeStruct((blocks, S, BLK), BF16),
            jax.ShapeDtypeStruct((blocks, 3 * SLOTS), jnp.int32),
            jax.ShapeDtypeStruct((3, blocks), jnp.int32),
        ],
        in_specs=[smem, smem, vmem, vmem],
        out_specs=[vmem, vmem, smem, smem],
        compiler_params=params(),
        name="extend",
    )(child_map, pattern, child_samples, forward_probe)


def exchange_kernel(
    pattern_ref, prior_ref, final_ref, probe_ref, adjoint_ref, sent_ref, sparse_ref,
    samples_ref, gram_ref,
    ext, before, after, down, up, above, below, sums, blocks, samples, gram, packed, partner,
    ext_send, ext_recv, row_send, row_recv, quad_send, quad_recv, local_sem, block_sem,
):
    row = lax.axis_index("row")
    col = lax.axis_index("col")
    n_row = lax.axis_size("row")
    n_col = lax.axis_size("col")
    n_blocks = blocks.shape[0]
    side = 4
    cx = col // side
    cy = col % side
    inner_up = row < n_row - 1
    inner_down = row > 0

    peers = []
    for d in range(1, n_col):
        px = (cx + d // side) % side
        py = (cy + d % side) % side
        peers.append(px * side + py)

    barrier = pltpu.get_barrier_semaphore()
    for peer in peers:
        pl.semaphore_signal(barrier, inc=1, device_id=(row, peer), device_id_type=MESH)

    for neighbour in ((row + 1) % n_row, (row + n_row - 1) % n_row):
        pl.semaphore_signal(barrier, inc=1, device_id=(neighbour, col), device_id_type=MESH)

    fetches = [
        pltpu.make_async_copy(sparse_ref.at[b], blocks.at[b], block_sem.at[b])
        for b in range(n_blocks)
    ]
    ext_fetch = pltpu.make_async_copy(sent_ref.at[col], ext.at[col], local_sem.at[1])
    for fetch in fetches:
        fetch.start()
    ext_fetch.start()

    @pl.when(row == 0)
    def _():
        before[...] = jnp.zeros_like(before)
        up[...] = jnp.zeros_like(up)

    @pl.when(row == n_row - 1)
    def _():
        after[...] = jnp.zeros_like(after)
        down[...] = jnp.zeros_like(down)

    def to_row(source, target, index, step):
        return pltpu.make_async_remote_copy(
            src_ref=source,
            dst_ref=target,
            send_sem=row_send.at[index],
            recv_sem=row_recv.at[index],
            device_id=(row + step, col),
            device_id_type=MESH,
        )

    rising = [to_row(probe_ref, before, 0, 1), to_row(below, up, 1, 1)]
    falling = [to_row(probe_ref, after, 2, -1), to_row(above, down, 3, -1)]

    none = n_blocks * SLOTS
    for q in range(3):
        sums[q, none] = jnp.zeros((S, BLK), F32)
    def adjoint_regions(regions, begin, end):
        def step(b, carry):
            probe = adjoint_ref[:, pl.ds(pl.multiple_of(b * BLK, BLK), BLK)]
            for s in range(0, SLOTS, 2):
                for q in regions:
                    slot = q * SLOTS + s
                    pair = jnp.concatenate([blocks[b, slot], blocks[b, slot + 1]], axis=1)
                    product = jnp.dot(probe, pair, preferred_element_type=F32)
                    for i in range(2):
                        sums[q, b * SLOTS + s + i] = (
                            product[:, i * BLK : (i + 1) * BLK]
                            + sums[q, prior_ref[b, slot + i]]
                        )
            return carry

        lax.fori_loop(begin, end, step, 0)

    early = 3 * n_blocks // 4
    for fetch in fetches[:early]:
        fetch.wait()
    adjoint_regions((0, 2), 0, early)
    pl.semaphore_wait(barrier, n_col + 1)

    @pl.when(inner_up)
    def _():
        rising[0].start()

    @pl.when(inner_down)
    def _():
        falling[0].start()

    spread = [
        pltpu.make_async_remote_copy(
            src_ref=sent_ref.at[peer, k],
            dst_ref=ext.at[col, k],
            send_sem=ext_send.at[k, i],
            recv_sem=ext_recv.at[k, i],
            device_id=(row, peer),
            device_id_type=MESH,
        )
        for k in range(2)
        for i, peer in enumerate(peers)
    ]
    for copy in spread:
        copy.start()

    def product(b, regions):
        left = []
        right = []
        for q, source in regions:
            for s in range(q * SLOTS, (q + 1) * SLOTS):
                left.append(source[pattern_ref[row, b, s]])
                right.append(blocks[b, s])
        return lax.dot_general(
            jnp.concatenate(left, axis=1),
            jnp.concatenate(right, axis=1),
            (((1,), (1,)), ((), ())),
            preferred_element_type=F32,
        )

    for fetch in fetches[early:]:
        fetch.wait()
    adjoint_regions((0, 2), early, n_blocks)

    def settle(c, carry):
        above[c] = sums[0, final_ref[0, c]].astype(BF16)
        below[c] = sums[2, final_ref[2, c]].astype(BF16)
        return carry

    lax.fori_loop(0, n_blocks, settle, 0)

    @pl.when(inner_up)
    def _():
        rising[1].start()

    @pl.when(inner_down)
    def _():
        falling[1].start()

    def own_region(b, carry):
        lanes = pl.ds(pl.multiple_of(b * BLK, BLK), BLK)
        samples[0, :, lanes] = product(b, [(1, probe_ref)])
        return carry

    lax.fori_loop(0, n_blocks, own_region, 0)

    @pl.when(inner_down)
    def _():
        rising[0].wait_recv()

    @pl.when(inner_up)
    def _():
        falling[0].wait_recv()

    def other_regions(b, carry):
        lanes = pl.ds(pl.multiple_of(b * BLK, BLK), BLK)
        samples[0, :, lanes] += product(b, [(0, before), (2, after)])
        return carry

    lax.fori_loop(0, n_blocks, other_regions, 0)

    gram[...] = jnp.zeros_like(gram)
    row_id = lax.broadcasted_iota(jnp.int32, (BLK, BLK), 0)
    col_id = lax.broadcasted_iota(jnp.int32, (BLK, BLK), 1)
    quad = []

    def finish(k, other_terms):
        def assemble(h, carry):
            lanes = pl.ds(pl.multiple_of(h * 2 * BLK, 2 * BLK), 2 * BLK)
            y = ext[:, k, :, lanes].reshape(S, 2 * BLK).astype(F32) + other_terms(h, lanes)
            samples[k, :, lanes] = y
            gram[k] += dot3(y, y, ((1,), (1,)))
            return carry

        lax.fori_loop(0, n_blocks // 2, assemble, 0)
        last = gram[k, BLK:, BLK:]
        diagonal = jnp.sum(jnp.where(row_id == col_id, last, 0.0), axis=0, keepdims=True)
        pieces = (
            (0, gram[k, :BLK, BLK:]),
            (BLK, jnp.where(col_id >= row_id, gram[k, :BLK, :BLK], last)),
            (2 * BLK, jnp.broadcast_to(diagonal, (16, BLK))),
        )
        for at, piece in pieces:
            gram_ref[0, k, at : at + piece.shape[0]] = piece
            packed[k, at : at + piece.shape[0]] = piece.astype(BF16)
        copies = [
            pltpu.make_async_remote_copy(
                src_ref=packed.at[k],
                dst_ref=partner.at[i, k],
                send_sem=quad_send.at[3 * k + i],
                recv_sem=quad_recv.at[3 * k + i],
                device_id=(row, cx * side + other),
                device_id_type=MESH,
            )
            for i, other in enumerate((cy + 1 - 2 * (cy % 2), (cy + 2) % side, side - 1 - cy))
        ]
        for copy in copies:
            copy.start()
        quad.append(copies)

    ext_fetch.wait()
    for copy in spread[: n_col - 1]:
        copy.wait_recv()
    finish(0, lambda h, lanes: samples[0, :, lanes])
    adjoint_regions((1,), 0, n_blocks)
    for copy in spread[n_col - 1 :]:
        copy.wait_recv()

    @pl.when(inner_down)
    def _():
        rising[1].wait_recv()

    @pl.when(inner_up)
    def _():
        falling[1].wait_recv()

    def adjoint_terms(h, lanes):
        parts = []
        for c in range(2):
            at = h * 2 + c
            parts.append(sums[1, final_ref[1, at]] + down[at].astype(F32) + up[at].astype(F32))
        return jnp.concatenate(parts, axis=1)

    finish(1, adjoint_terms)
    store = pltpu.make_async_copy(samples, samples_ref, local_sem.at[2])
    store.start()

    @pl.when(inner_up)
    def _():
        for copy in rising:
            copy.wait_send()

    @pl.when(inner_down)
    def _():
        for copy in falling:
            copy.wait_send()

    for copy in spread:
        copy.wait_send()
    for k in range(2):
        quad[k][0].wait_recv()
        gram_ref[1, k] = gram_ref[0, k] + partner[0, k].astype(F32)
        quad[k][1].wait_recv()
        quad[k][2].wait_recv()
        gram_ref[2, k] = gram_ref[1, k] + partner[1, k].astype(F32) + partner[2, k].astype(F32)
    for copies in quad:
        for copy in copies:
            copy.wait_send()
    store.wait()


def exchange(pattern, prior, final, probe, adjoint_probe, sent, sparse):
    rows = sent.shape[3]
    leaves = sent.shape[0]
    held = 2 * BLK + 16
    anywhere = pl.BlockSpec(memory_space=pl.ANY)
    vmem = pl.BlockSpec(memory_space=pltpu.VMEM)
    dma = pltpu.SemaphoreType.DMA
    return pl.pallas_call(
        exchange_kernel,
        out_shape=[
            jax.ShapeDtypeStruct((2, S, rows), F32),
            jax.ShapeDtypeStruct((3, 2, held, BLK), F32),
        ],
        in_specs=[pl.BlockSpec(memory_space=pltpu.SMEM)] * 3 + [vmem] * 2 + [anywhere] * 2,
        out_specs=[anywhere, vmem],
        scratch_shapes=[
            pltpu.VMEM(sent.shape, BF16),
            pltpu.VMEM(probe.shape, BF16),
            pltpu.VMEM(probe.shape, BF16),
            pltpu.VMEM(probe.shape, BF16),
            pltpu.VMEM(probe.shape, BF16),
            pltpu.VMEM(probe.shape, BF16),
            pltpu.VMEM(probe.shape, BF16),
            pltpu.VMEM((3, sparse.shape[0] * SLOTS + 1, S, BLK), F32),
            pltpu.VMEM(sparse.shape, BF16),
            pltpu.VMEM((2, S, rows), F32),
            pltpu.VMEM((2, S, S), F32),
            pltpu.VMEM((2, held, BLK), BF16),
            pltpu.VMEM((3, 2, held, BLK), BF16),
            dma((2, leaves - 1)),
            dma((2, leaves - 1)),
            dma((4,)),
            dma((4,)),
            dma((6,)),
            dma((6,)),
            dma((3,)),
            dma((sparse.shape[0],)),
        ],
        compiler_params=pltpu.CompilerParams(
            collective_id=0, has_side_effects=True, vmem_limit_bytes=VMEM_LIMIT
        ),
        name="exchange",
    )(pattern, prior, final, probe, adjoint_probe, sent, sparse)


def splat(x, at):
    return jnp.broadcast_to(x[:, at:at+1], (8, BLK))

def eliminate(rows, first, half, lane, others):
    count=len(rows)
    for g in range(0, count, SUB):
        base=first+g
        e=[[splat(rows[g+j][half], base+i) if i>=j else None for i in range(SUB)] for j in range(SUB)]
        scale=[]; fac=[]
        for j in range(SUB):
            s=lax.rsqrt(e[j][j]); scale.append(s)
            f=[e[j][i]*s if i>j else None for i in range(SUB)]
            fac.append(f)
            for i in range(j+1,SUB):
                for l in range(i,SUB):
                    e[i][l]=e[i][l]-f[i]*f[l]
        share=-(-len(others)*SUB//(count-g))
        for other in others[:share]:
            other()
        others=others[share:]
        clean=[]
        for j in range(SUB):
            here=lane==base+j
            z=[x*scale[j] for x in rows[g+j]]
            z[half]=jnp.where(here,scale[j],z[half])
            rows[g+j]=z
            for i in range(j+1,SUB):
                r=list(rows[g+i]); r[half]=jnp.where(here,0.0,r[half])
                rows[g+i]=[x-fac[j][i]*y for x,y in zip(r,z)]
            c=list(z); c[half]=jnp.where((lane>base+j)&(lane<base+SUB),0.0,z[half]); clean.append(c)
        for i in range(g+SUB,count):
            r=list(rows[i]); r[half]=jnp.where((lane>=base)&(lane<base+SUB),0.0,r[half])
            for j in range(SUB):
                z=clean[j]
                f=splat(z[half], first+i)
                r=[x-f*y for x,y in zip(r,z)]
            rows[i]=r
    return rows

def factorize(work, count):
    lane = lax.broadcasted_iota(jnp.int32, (8, BLK), 1)
    others = []
    for lo in range(0, S, PANEL):
        half = lo // BLK
        rows = [
            [work[b][pl.ds(lo + i, 8, stride=PITCH), :] for b in range(2)] for i in range(PANEL)
        ]
        rows = eliminate(rows, lo - half * BLK, half, lane, others)
        for i in range(PANEL):
            for b in range(2):
                work[b][pl.ds(lo + i, 8, stride=PITCH), :] = rows[i][b]
        end = lo + PANEL
        if end == S:
            break
        skip = end // BLK
        row_id = lax.broadcasted_iota(jnp.int32, (PANEL, BLK), 0) + lo
        col_id = lax.broadcasted_iota(jnp.int32, (PANEL, BLK), 1) + BLK * half
        dead = (col_id > row_id) & (col_id < end)
        operands = []
        for m in range(count):
            base = m * PITCH
            panel = [work[b][base + lo : base + end, :] for b in range(2)]
            masked = [jnp.where(dead, 0.0, x) if b == half else x for b, x in enumerate(panel)]
            left = panel[1] if skip else jnp.concatenate(panel, axis=1)
            lh, lm, ll = split3(left)
            rh, rm, rl = split3(jnp.concatenate(masked, axis=1))
            operands.append(
                (
                    jnp.concatenate([lh, lh, lm, lh, ll, lm], axis=0).T,
                    jnp.concatenate([rh, rm, rh, rl, rh, rm], axis=0),
                )
            )

        def update(m, begin, stop, lo=lo, end=end, half=half, skip=skip, operands=operands):
            left, right = operands[m]
            product = jnp.dot(
                left[begin - skip * BLK : stop - skip * BLK], right, preferred_element_type=F32
            )
            cols = lax.broadcasted_iota(jnp.int32, (stop - begin, BLK), 1) + BLK * half
            mine = (cols >= lo) & (cols < end)
            base = m * PITCH
            for b in range(2):
                old = work[b][base + begin : base + stop, :]
                if b == half:
                    old = jnp.where(mine, 0.0, old)
                work[b][base + begin : base + stop, :] = old - product[:, b * BLK : (b + 1) * BLK]

        near = end + PANEL
        for m in range(count):
            update(m, end, near)
        others = []
        if near < S:
            others = [partial(update, m, near, S) for m in range(count)]


def load_grams(gram_ref, work):
    w0, w1 = work
    corner_row = lax.broadcasted_iota(jnp.int32, (BLK, BLK), 0)
    corner_col = lax.broadcasted_iota(jnp.int32, (BLK, BLK), 1)
    for m in range(8):
        held = gram_ref.at[m // 2 % 3, m % 2]
        shared = held[BLK : 2 * BLK]
        at = m * PITCH
        w0[at : at + BLK, :] = shared
        w1[at : at + BLK, :] = held[:BLK]
        w1[at + BLK : at + S, :] = jnp.where(
            corner_row == corner_col,
            jnp.broadcast_to(held[2 * BLK : 2 * BLK + 1], (BLK, BLK)),
            shared.T,
        )
        w0[at + BLK : at + S, :] = jnp.zeros((BLK, BLK), F32)


def factor_kernel(gram_ref, samples_ref, row_ref, col_ref, transfer_ref, w0, w1):
    work = (w0, w1)
    load_grams(gram_ref, work)
    factorize(work, 6)
    row_id = lax.broadcasted_iota(jnp.int32, (S, S), 0)
    col_id = lax.broadcasted_iota(jnp.int32, (S, S), 1)
    gain = math.sqrt(samples_ref.shape[2])
    for k in range(2):
        found = []
        for level in range(3):
            at = (2 * level + k) * PITCH
            found.append(jnp.concatenate([work[b][at : at + S, :] for b in range(2)], axis=1))
        inverse = [jnp.where(col_id <= row_id, x, 0.0) for x in found]
        upper = [
            jnp.where(col_id > row_id, x, jnp.where(col_id == row_id, 1.0 / x, 0.0))
            for x in found[:2]
        ]
        basis = dot3(inverse[0], samples_ref[k], ((1,), (0,))) * gain
        (row_ref, col_ref)[k][...] = basis.astype(BF16)
        for level in range(2):
            transfer_ref[k, level] = dot3(upper[level], inverse[level + 1], ((1,), (1,)))


def factor(grams, samples):
    rows = samples.shape[2]
    vmem = pl.BlockSpec(memory_space=pltpu.VMEM)
    return pl.pallas_call(
        factor_kernel,
        out_shape=[
            jax.ShapeDtypeStruct((S, rows), BF16),
            jax.ShapeDtypeStruct((S, rows), BF16),
            jax.ShapeDtypeStruct((2, 2, S, S), F32),
        ],
        in_specs=[vmem] * 2,
        out_specs=[vmem] * 3,
        scratch_shapes=[pltpu.VMEM((8 * PITCH, BLK), F32)] * 2,
        compiler_params=params(),
        name="factor",
    )(grams, samples)


def local(
    child_samples, child_map, forward_probe, adjoint_probe, stored_sparse_blocks, block_pattern
):
    leaves = lax.axis_size("col")
    sent, blocked, prior, final = extend(
        child_map, block_pattern, child_samples, forward_probe, leaves
    )
    samples, grams = exchange(
        block_pattern, prior, final, blocked, adjoint_probe, sent, stored_sparse_blocks
    )
    return tuple(factor(grams, samples))


def solution(mesh):
    return jax.shard_map(
        local,
        mesh=mesh,
        in_specs=(
            P(None, None, "col", "row"),
            P(None, "row"),
            P(None, ("row", "col")),
            P(None, ("row", "col")),
            P(("row", "col"), None, None, None),
            P(None, "col", None),
        ),
        out_specs=(
            P(None, ("row", "col")),
            P(None, ("row", "col")),
            P(None, None, ("row", "col"), None),
        ),
        check_vma=False,
    )
```

```python
from functools import partial
import math

import jax
import jax.numpy as jnp
from jax import lax
from jax.experimental import pallas as pl
from jax.experimental.pallas import tpu as pltpu
from jax.sharding import PartitionSpec as P

S = 256
BLK = 128
SLOTS = 6
PANEL = 16
SUB = 8
PITCH = S + 8
F32 = jnp.float32
BF16 = jnp.bfloat16
MESH = pl.DeviceIdType.MESH
VMEM_LIMIT = 56 << 20


def params():
    return pltpu.CompilerParams(vmem_limit_bytes=VMEM_LIMIT)


def split3(x):
    high = x.astype(BF16)
    rest = x - high.astype(F32)
    mid = rest.astype(BF16)
    low = (rest - mid.astype(F32)).astype(BF16)
    return high, mid, low


def dot3(a, b, dims):
    ah, am, _ = split3(a)
    bh, bm, _ = split3(b)
    dn = (dims, ((), ()))
    out = lax.dot_general(ah, bh, dn, preferred_element_type=F32)
    out += lax.dot_general(ah, bm, dn, preferred_element_type=F32)
    out += lax.dot_general(am, bh, dn, preferred_element_type=F32)
    return out


def extend_kernel(
    map_ref, pattern_ref, child_ref, forward_ref, sent_ref, blocked_ref, prior_ref, final_ref,
    child, child_sem,
):
    row = lax.axis_index("row")
    leaves = sent_ref.shape[0]
    blocks = blocked_ref.shape[0]
    none = blocks * SLOTS
    fetches = [
        pltpu.make_async_copy(child_ref.at[:, k], child.at[k], child_sem.at[k]) for k in range(2)
    ]
    for fetch in fetches:
        fetch.start()
    for q in range(3):
        for c in range(blocks):
            final_ref[q, c] = none
    for b in range(blocks):
        blocked_ref[b] = forward_ref[:, b * BLK : (b + 1) * BLK]

    def link(b, s):
        q = s // SLOTS
        target = pattern_ref[row, b, s]
        prior_ref[b, s] = final_ref[q, target]
        final_ref[q, target] = b * SLOTS + s - q * SLOTS

    def leaf(k, d):
        for c in range(blocks):
            first = pl.multiple_of(map_ref[0, d * blocks + c] * BLK, BLK)
            second = pl.multiple_of(map_ref[1, d * blocks + c] * BLK, BLK)
            x = child[k, 0, :, pl.ds(first, BLK)].astype(F32)
            y = child[k, 1, :, pl.ds(second, BLK)].astype(F32)
            sent_ref[d, k, :, c * BLK : (c + 1) * BLK] = (x + y).astype(BF16)

    def first_half(i, carry):
        for s in range(3 * SLOTS):
            link(i, s)
        for part in range(leaves // blocks):
            leaf(0, i + part * blocks)
        return carry

    def second_half(i, carry):
        for part in range(leaves // blocks):
            leaf(1, i + part * blocks)
        return carry

    fetches[0].wait()
    lax.fori_loop(0, blocks, first_half, 0)
    fetches[1].wait()
    lax.fori_loop(0, blocks, second_half, 0)


def extend(child_map, pattern, child_samples, forward_probe, leaves):
    samples_here, rows_group = child_samples.shape[2:]
    rows = forward_probe.shape[1]
    blocks = rows // BLK
    smem = pl.BlockSpec(memory_space=pltpu.SMEM)
    vmem = pl.BlockSpec(memory_space=pltpu.VMEM)
    return pl.pallas_call(
        extend_kernel,
        out_shape=[
            jax.ShapeDtypeStruct((leaves, 2, samples_here, rows_group // leaves), BF16),
            jax.ShapeDtypeStruct((blocks, S, BLK), BF16),
            jax.ShapeDtypeStruct((blocks, 3 * SLOTS), jnp.int32),
            jax.ShapeDtypeStruct((3, blocks), jnp.int32),
        ],
        in_specs=[smem, smem, pl.BlockSpec(memory_space=pl.ANY), vmem],
        out_specs=[vmem, vmem, smem, smem],
        scratch_shapes=[
            pltpu.VMEM(child_samples.shape, BF16),
            pltpu.SemaphoreType.DMA((2,)),
        ],
        compiler_params=params(),
        name="extend",
    )(child_map, pattern, child_samples, forward_probe)


def exchange_kernel(
    pattern_ref, prior_ref, final_ref, probe_ref, adjoint_ref, sent_ref, sparse_ref,
    samples_ref, gram_ref,
    ext, before, after, down, up, above, below, sums, blocks, samples, gram, packed, partner,
    ext_send, ext_recv, row_send, row_recv, quad_send, quad_recv, local_sem, block_sem,
):
    row = lax.axis_index("row")
    col = lax.axis_index("col")
    n_row = lax.axis_size("row")
    n_col = lax.axis_size("col")
    n_blocks = blocks.shape[0]
    side = 4
    cx = col // side
    cy = col % side
    inner_up = row < n_row - 1
    inner_down = row > 0

    peers = []
    for d in range(1, n_col):
        px = (cx + d // side) % side
        py = (cy + d % side) % side
        peers.append(px * side + py)

    barrier = pltpu.get_barrier_semaphore()
    for peer in peers:
        pl.semaphore_signal(barrier, inc=1, device_id=(row, peer), device_id_type=MESH)

    for neighbour in ((row + 1) % n_row, (row + n_row - 1) % n_row):
        pl.semaphore_signal(barrier, inc=1, device_id=(neighbour, col), device_id_type=MESH)

    fetches = [
        pltpu.make_async_copy(sparse_ref.at[b], blocks.at[b], block_sem.at[b])
        for b in range(n_blocks)
    ]
    ext_fetch = pltpu.make_async_copy(sent_ref.at[col], ext.at[col], local_sem.at[1])
    for fetch in fetches:
        fetch.start()
    ext_fetch.start()

    @pl.when(row == 0)
    def _():
        before[...] = jnp.zeros_like(before)
        up[...] = jnp.zeros_like(up)

    @pl.when(row == n_row - 1)
    def _():
        after[...] = jnp.zeros_like(after)
        down[...] = jnp.zeros_like(down)

    def to_row(source, target, index, step):
        return pltpu.make_async_remote_copy(
            src_ref=source,
            dst_ref=target,
            send_sem=row_send.at[index],
            recv_sem=row_recv.at[index],
            device_id=(row + step, col),
            device_id_type=MESH,
        )

    rising = [to_row(probe_ref, before, 0, 1), to_row(below, up, 1, 1)]
    falling = [to_row(probe_ref, after, 2, -1), to_row(above, down, 3, -1)]

    none = n_blocks * SLOTS
    for q in range(3):
        sums[q, none] = jnp.zeros((S, BLK), F32)
    def adjoint_regions(regions, begin, end):
        def step(b, carry):
            probe = adjoint_ref[:, pl.ds(pl.multiple_of(b * BLK, BLK), BLK)]
            for s in range(0, SLOTS, 2):
                for q in regions:
                    slot = q * SLOTS + s
                    pair = jnp.concatenate([blocks[b, slot], blocks[b, slot + 1]], axis=1)
                    product = jnp.dot(probe, pair, preferred_element_type=F32)
                    for i in range(2):
                        sums[q, b * SLOTS + s + i] = (
                            product[:, i * BLK : (i + 1) * BLK]
                            + sums[q, prior_ref[b, slot + i]]
                        )
            return carry

        lax.fori_loop(begin, end, step, 0)

    early = n_blocks // 4
    for fetch in fetches[:early]:
        fetch.wait()
    adjoint_regions((0, 2), 0, early)
    pl.semaphore_wait(barrier, n_col + 1)

    @pl.when(inner_up)
    def _():
        rising[0].start()

    @pl.when(inner_down)
    def _():
        falling[0].start()

    spread = [
        pltpu.make_async_remote_copy(
            src_ref=sent_ref.at[peer, k],
            dst_ref=ext.at[col, k],
            send_sem=ext_send.at[k, i],
            recv_sem=ext_recv.at[k, i],
            device_id=(row, peer),
            device_id_type=MESH,
        )
        for k in range(2)
        for i, peer in enumerate(peers)
    ]
    for copy in spread:
        copy.start()

    def product(b, regions):
        left = []
        right = []
        for q, source in regions:
            for s in range(q * SLOTS, (q + 1) * SLOTS):
                left.append(source[pattern_ref[row, b, s]])
                right.append(blocks[b, s])
        return lax.dot_general(
            jnp.concatenate(left, axis=1),
            jnp.concatenate(right, axis=1),
            (((1,), (1,)), ((), ())),
            preferred_element_type=F32,
        )

    for fetch in fetches[early:]:
        fetch.wait()
    adjoint_regions((0, 2), early, n_blocks)

    def settle(c, carry):
        above[c] = sums[0, final_ref[0, c]].astype(BF16)
        below[c] = sums[2, final_ref[2, c]].astype(BF16)
        return carry

    lax.fori_loop(0, n_blocks, settle, 0)

    @pl.when(inner_up)
    def _():
        rising[1].start()

    @pl.when(inner_down)
    def _():
        falling[1].start()

    def own_region(b, carry):
        lanes = pl.ds(pl.multiple_of(b * BLK, BLK), BLK)
        samples[0, :, lanes] = product(b, [(1, probe_ref)])
        return carry

    lax.fori_loop(0, n_blocks, own_region, 0)

    @pl.when(inner_down)
    def _():
        rising[0].wait_recv()

    @pl.when(inner_up)
    def _():
        falling[0].wait_recv()

    def other_regions(b, carry):
        lanes = pl.ds(pl.multiple_of(b * BLK, BLK), BLK)
        samples[0, :, lanes] += product(b, [(0, before), (2, after)])
        return carry

    lax.fori_loop(0, n_blocks, other_regions, 0)

    gram[...] = jnp.zeros_like(gram)
    row_id = lax.broadcasted_iota(jnp.int32, (BLK, BLK), 0)
    col_id = lax.broadcasted_iota(jnp.int32, (BLK, BLK), 1)
    quad = []

    def finish(k, other_terms):
        def assemble(h, carry):
            lanes = pl.ds(pl.multiple_of(h * 2 * BLK, 2 * BLK), 2 * BLK)
            y = ext[:, k, :, lanes].reshape(S, 2 * BLK).astype(F32) + other_terms(h, lanes)
            samples[k, :, lanes] = y
            gram[k] += dot3(y, y, ((1,), (1,)))
            return carry

        lax.fori_loop(0, n_blocks // 2, assemble, 0)
        last = gram[k, BLK:, BLK:]
        diagonal = jnp.sum(jnp.where(row_id == col_id, last, 0.0), axis=0, keepdims=True)
        pieces = (
            (0, gram[k, :BLK, BLK:]),
            (BLK, jnp.where(col_id >= row_id, gram[k, :BLK, :BLK], last)),
            (2 * BLK, jnp.broadcast_to(diagonal, (16, BLK))),
        )
        for at, piece in pieces:
            gram_ref[0, k, at : at + piece.shape[0]] = piece
            packed[k, at : at + piece.shape[0]] = piece.astype(BF16)
        copies = [
            pltpu.make_async_remote_copy(
                src_ref=packed.at[k],
                dst_ref=partner.at[i, k],
                send_sem=quad_send.at[3 * k + i],
                recv_sem=quad_recv.at[3 * k + i],
                device_id=(row, cx * side + other),
                device_id_type=MESH,
            )
            for i, other in enumerate((cy + 1 - 2 * (cy % 2), (cy + 2) % side, side - 1 - cy))
        ]
        for copy in copies:
            copy.start()
        quad.append(copies)

    ext_fetch.wait()
    for copy in spread[: n_col - 1]:
        copy.wait_recv()
    finish(0, lambda h, lanes: samples[0, :, lanes])
    adjoint_regions((1,), 0, n_blocks)
    for copy in spread[n_col - 1 :]:
        copy.wait_recv()

    @pl.when(inner_down)
    def _():
        rising[1].wait_recv()

    @pl.when(inner_up)
    def _():
        falling[1].wait_recv()

    def adjoint_terms(h, lanes):
        parts = []
        for c in range(2):
            at = h * 2 + c
            parts.append(sums[1, final_ref[1, at]] + down[at].astype(F32) + up[at].astype(F32))
        return jnp.concatenate(parts, axis=1)

    finish(1, adjoint_terms)
    store = pltpu.make_async_copy(samples, samples_ref, local_sem.at[2])
    store.start()

    @pl.when(inner_up)
    def _():
        for copy in rising:
            copy.wait_send()

    @pl.when(inner_down)
    def _():
        for copy in falling:
            copy.wait_send()

    for copy in spread:
        copy.wait_send()
    for k in range(2):
        quad[k][0].wait_recv()
        gram_ref[1, k] = gram_ref[0, k] + partner[0, k].astype(F32)
        quad[k][1].wait_recv()
        quad[k][2].wait_recv()
        gram_ref[2, k] = gram_ref[1, k] + partner[1, k].astype(F32) + partner[2, k].astype(F32)
    for copies in quad:
        for copy in copies:
            copy.wait_send()
    store.wait()


def exchange(pattern, prior, final, probe, adjoint_probe, sent, sparse):
    rows = sent.shape[3]
    leaves = sent.shape[0]
    held = 2 * BLK + 16
    anywhere = pl.BlockSpec(memory_space=pl.ANY)
    vmem = pl.BlockSpec(memory_space=pltpu.VMEM)
    dma = pltpu.SemaphoreType.DMA
    return pl.pallas_call(
        exchange_kernel,
        out_shape=[
            jax.ShapeDtypeStruct((2, S, rows), F32),
            jax.ShapeDtypeStruct((3, 2, held, BLK), F32),
        ],
        in_specs=[pl.BlockSpec(memory_space=pltpu.SMEM)] * 3 + [vmem] * 2 + [anywhere] * 2,
        out_specs=[anywhere, vmem],
        scratch_shapes=[
            pltpu.VMEM(sent.shape, BF16),
            pltpu.VMEM(probe.shape, BF16),
            pltpu.VMEM(probe.shape, BF16),
            pltpu.VMEM(probe.shape, BF16),
            pltpu.VMEM(probe.shape, BF16),
            pltpu.VMEM(probe.shape, BF16),
            pltpu.VMEM(probe.shape, BF16),
            pltpu.VMEM((3, sparse.shape[0] * SLOTS + 1, S, BLK), F32),
            pltpu.VMEM(sparse.shape, BF16),
            pltpu.VMEM((2, S, rows), F32),
            pltpu.VMEM((2, S, S), F32),
            pltpu.VMEM((2, held, BLK), BF16),
            pltpu.VMEM((3, 2, held, BLK), BF16),
            dma((2, leaves - 1)),
            dma((2, leaves - 1)),
            dma((4,)),
            dma((4,)),
            dma((6,)),
            dma((6,)),
            dma((3,)),
            dma((sparse.shape[0],)),
        ],
        compiler_params=pltpu.CompilerParams(
            collective_id=0, has_side_effects=True, vmem_limit_bytes=VMEM_LIMIT
        ),
        name="exchange",
    )(pattern, prior, final, probe, adjoint_probe, sent, sparse)


def splat(x, at):
    return jnp.broadcast_to(x[:, at:at+1], (8, BLK))

def eliminate(rows, first, half, lane, others):
    count=len(rows)
    for g in range(0, count, SUB):
        base=first+g
        e=[[splat(rows[g+j][half], base+i) if i>=j else None for i in range(SUB)] for j in range(SUB)]
        scale=[]; fac=[]
        for j in range(SUB):
            s=lax.rsqrt(e[j][j]); scale.append(s)
            f=[e[j][i]*s if i>j else None for i in range(SUB)]
            fac.append(f)
            for i in range(j+1,SUB):
                for l in range(i,SUB):
                    e[i][l]=e[i][l]-f[i]*f[l]
        share=-(-len(others)*SUB//(count-g))
        for other in others[:share]:
            other()
        others=others[share:]
        clean=[]
        for j in range(SUB):
            here=lane==base+j
            z=[x*scale[j] for x in rows[g+j]]
            z[half]=jnp.where(here,scale[j],z[half])
            rows[g+j]=z
            for i in range(j+1,SUB):
                r=list(rows[g+i]); r[half]=jnp.where(here,0.0,r[half])
                rows[g+i]=[x-fac[j][i]*y for x,y in zip(r,z)]
            c=list(z); c[half]=jnp.where((lane>base+j)&(lane<base+SUB),0.0,z[half]); clean.append(c)
        for i in range(g+SUB,count):
            r=list(rows[i]); r[half]=jnp.where((lane>=base)&(lane<base+SUB),0.0,r[half])
            for j in range(SUB):
                z=clean[j]
                f=splat(z[half], first+i)
                r=[x-f*y for x,y in zip(r,z)]
            rows[i]=r
    return rows

def factorize(work, count):
    lane = lax.broadcasted_iota(jnp.int32, (8, BLK), 1)
    others = []
    for lo in range(0, S, PANEL):
        half = lo // BLK
        rows = [
            [work[b][pl.ds(lo + i, 8, stride=PITCH), :] for b in range(2)] for i in range(PANEL)
        ]
        rows = eliminate(rows, lo - half * BLK, half, lane, others)
        for i in range(PANEL):
            for b in range(2):
                work[b][pl.ds(lo + i, 8, stride=PITCH), :] = rows[i][b]
        end = lo + PANEL
        if end == S:
            break
        skip = end // BLK
        row_id = lax.broadcasted_iota(jnp.int32, (PANEL, BLK), 0) + lo
        col_id = lax.broadcasted_iota(jnp.int32, (PANEL, BLK), 1) + BLK * half
        dead = (col_id > row_id) & (col_id < end)
        operands = []
        for m in range(count):
            base = m * PITCH
            panel = [work[b][base + lo : base + end, :] for b in range(2)]
            masked = [jnp.where(dead, 0.0, x) if b == half else x for b, x in enumerate(panel)]
            left = panel[1] if skip else jnp.concatenate(panel, axis=1)
            lh, lm, ll = split3(left)
            rh, rm, rl = split3(jnp.concatenate(masked, axis=1))
            operands.append(
                (
                    jnp.concatenate([lh, lh, lm, lh, ll, lm], axis=0).T,
                    jnp.concatenate([rh, rm, rh, rl, rh, rm], axis=0),
                )
            )

        def update(m, begin, stop, lo=lo, end=end, half=half, skip=skip, operands=operands):
            left, right = operands[m]
            product = jnp.dot(
                left[begin - skip * BLK : stop - skip * BLK], right, preferred_element_type=F32
            )
            cols = lax.broadcasted_iota(jnp.int32, (stop - begin, BLK), 1) + BLK * half
            mine = (cols >= lo) & (cols < end)
            base = m * PITCH
            for b in range(2):
                old = work[b][base + begin : base + stop, :]
                if b == half:
                    old = jnp.where(mine, 0.0, old)
                work[b][base + begin : base + stop, :] = old - product[:, b * BLK : (b + 1) * BLK]

        near = end + PANEL
        for m in range(count):
            update(m, end, near)
        others = []
        if near < S:
            others = [partial(update, m, near, S) for m in range(count)]


def load_grams(gram_ref, work):
    w0, w1 = work
    corner_row = lax.broadcasted_iota(jnp.int32, (BLK, BLK), 0)
    corner_col = lax.broadcasted_iota(jnp.int32, (BLK, BLK), 1)
    for m in range(8):
        held = gram_ref.at[m // 2 % 3, m % 2]
        shared = held[BLK : 2 * BLK]
        at = m * PITCH
        w0[at : at + BLK, :] = shared
        w1[at : at + BLK, :] = held[:BLK]
        w1[at + BLK : at + S, :] = jnp.where(
            corner_row == corner_col,
            jnp.broadcast_to(held[2 * BLK : 2 * BLK + 1], (BLK, BLK)),
            shared.T,
        )
        w0[at + BLK : at + S, :] = jnp.zeros((BLK, BLK), F32)


def factor_kernel(gram_ref, samples_ref, row_ref, col_ref, transfer_ref, w0, w1):
    work = (w0, w1)
    load_grams(gram_ref, work)
    factorize(work, 6)
    row_id = lax.broadcasted_iota(jnp.int32, (S, S), 0)
    col_id = lax.broadcasted_iota(jnp.int32, (S, S), 1)
    gain = math.sqrt(samples_ref.shape[2])
    for k in range(2):
        found = []
        for level in range(3):
            at = (2 * level + k) * PITCH
            found.append(jnp.concatenate([work[b][at : at + S, :] for b in range(2)], axis=1))
        inverse = [jnp.where(col_id <= row_id, x, 0.0) for x in found]
        upper = [
            jnp.where(col_id > row_id, x, jnp.where(col_id == row_id, 1.0 / x, 0.0))
            for x in found[:2]
        ]
        basis = dot3(inverse[0], samples_ref[k], ((1,), (0,))) * gain
        (row_ref, col_ref)[k][...] = basis.astype(BF16)
        for level in range(2):
            transfer_ref[k, level] = dot3(upper[level], inverse[level + 1], ((1,), (1,)))


def factor(grams, samples):
    rows = samples.shape[2]
    vmem = pl.BlockSpec(memory_space=pltpu.VMEM)
    return pl.pallas_call(
        factor_kernel,
        out_shape=[
            jax.ShapeDtypeStruct((S, rows), BF16),
            jax.ShapeDtypeStruct((S, rows), BF16),
            jax.ShapeDtypeStruct((2, 2, S, S), F32),
        ],
        in_specs=[vmem] * 2,
        out_specs=[vmem] * 3,
        scratch_shapes=[pltpu.VMEM((8 * PITCH, BLK), F32)] * 2,
        compiler_params=params(),
        name="factor",
    )(grams, samples)


def local(
    child_samples, child_map, forward_probe, adjoint_probe, stored_sparse_blocks, block_pattern
):
    leaves = lax.axis_size("col")
    sent, blocked, prior, final = extend(
        child_map, block_pattern, child_samples, forward_probe, leaves
    )
    samples, grams = exchange(
        block_pattern, prior, final, blocked, adjoint_probe, sent, stored_sparse_blocks
    )
    return tuple(factor(grams, samples))


def solution(mesh):
    return jax.shard_map(
        local,
        mesh=mesh,
        in_specs=(
            P(None, None, "col", "row"),
            P(None, "row"),
            P(None, ("row", "col")),
            P(None, ("row", "col")),
            P(("row", "col"), None, None, None),
            P(None, "col", None),
        ),
        out_specs=(
            P(None, ("row", "col")),
            P(None, ("row", "col")),
            P(None, None, ("row", "col"), None),
        ),
        check_vma=False,
    )
```

```python
from functools import partial
import math

import jax
import jax.numpy as jnp
from jax import lax
from jax.experimental import pallas as pl
from jax.experimental.pallas import tpu as pltpu
from jax.sharding import PartitionSpec as P

S = 256
BLK = 128
SLOTS = 6
PANEL = 16
SUB = 8
PITCH = S + 8
F32 = jnp.float32
BF16 = jnp.bfloat16
MESH = pl.DeviceIdType.MESH
VMEM_LIMIT = 56 << 20


def params():
    return pltpu.CompilerParams(vmem_limit_bytes=VMEM_LIMIT)


def split3(x):
    high = x.astype(BF16)
    rest = x - high.astype(F32)
    mid = rest.astype(BF16)
    low = (rest - mid.astype(F32)).astype(BF16)
    return high, mid, low


def dot3(a, b, dims):
    ah, am, _ = split3(a)
    bh, bm, _ = split3(b)
    dn = (dims, ((), ()))
    out = lax.dot_general(ah, bh, dn, preferred_element_type=F32)
    out += lax.dot_general(ah, bm, dn, preferred_element_type=F32)
    out += lax.dot_general(am, bh, dn, preferred_element_type=F32)
    return out


def extend_kernel(
    map_ref, pattern_ref, child_ref, forward_ref, sent_ref, blocked_ref, prior_ref, final_ref
):
    row = lax.axis_index("row")
    leaves = sent_ref.shape[0]
    blocks = blocked_ref.shape[0]
    none = blocks * SLOTS
    for q in range(3):
        for c in range(blocks):
            final_ref[q, c] = none
    for b in range(blocks):
        blocked_ref[b] = forward_ref[:, b * BLK : (b + 1) * BLK]

    def link(b, s):
        q = s // SLOTS
        target = pattern_ref[row, b, s]
        prior_ref[b, s] = final_ref[q, target]
        final_ref[q, target] = b * SLOTS + s - q * SLOTS

    def leaf(d, carry):
        for c in range(blocks):
            first = pl.multiple_of(map_ref[0, d * blocks + c] * BLK, BLK)
            second = pl.multiple_of(map_ref[1, d * blocks + c] * BLK, BLK)
            for k in range(2):
                x = child_ref[0, k, :, pl.ds(first, BLK)].astype(F32)
                y = child_ref[1, k, :, pl.ds(second, BLK)].astype(F32)
                sent_ref[d, k, :, c * BLK : (c + 1) * BLK] = (x + y).astype(BF16)
        return carry

    def linked_leaf(d, carry):
        for s in range(3 * SLOTS):
            link(d, s)
        return leaf(d, carry)

    lax.fori_loop(0, blocks, linked_leaf, 0)
    lax.fori_loop(blocks, leaves, leaf, 0)


def extend(child_map, pattern, child_samples, forward_probe, leaves):
    samples_here, rows_group = child_samples.shape[2:]
    rows = forward_probe.shape[1]
    blocks = rows // BLK
    smem = pl.BlockSpec(memory_space=pltpu.SMEM)
    vmem = pl.BlockSpec(memory_space=pltpu.VMEM)
    return pl.pallas_call(
        extend_kernel,
        out_shape=[
            jax.ShapeDtypeStruct((leaves, 2, samples_here, rows_group // leaves), BF16),
            jax.ShapeDtypeStruct((blocks, S, BLK), BF16),
            jax.ShapeDtypeStruct((blocks, 3 * SLOTS), jnp.int32),
            jax.ShapeDtypeStruct((3, blocks), jnp.int32),
        ],
        in_specs=[smem, smem, vmem, vmem],
        out_specs=[vmem, vmem, smem, smem],
        compiler_params=params(),
        name="extend",
    )(child_map, pattern, child_samples, forward_probe)


def exchange_kernel(
    pattern_ref, prior_ref, final_ref, probe_ref, adjoint_ref, sent_ref, sparse_ref,
    samples_ref, gram_ref,
    ext, before, after, down, up, above, below, sums, blocks, samples, gram, packed, partner,
    ext_send, ext_recv, row_send, row_recv, quad_send, quad_recv, local_sem, block_sem,
):
    row = lax.axis_index("row")
    col = lax.axis_index("col")
    n_row = lax.axis_size("row")
    n_col = lax.axis_size("col")
    n_blocks = blocks.shape[0]
    side = 4
    cx = col // side
    cy = col % side
    inner_up = row < n_row - 1
    inner_down = row > 0

    peers = []
    for d in range(1, n_col):
        px = (cx + d // side) % side
        py = (cy + d % side) % side
        peers.append(px * side + py)

    barrier = pltpu.get_barrier_semaphore()
    for peer in peers:
        pl.semaphore_signal(barrier, inc=1, device_id=(row, peer), device_id_type=MESH)

    for neighbour in ((row + 1) % n_row, (row + n_row - 1) % n_row):
        pl.semaphore_signal(barrier, inc=1, device_id=(neighbour, col), device_id_type=MESH)

    fetches = [
        pltpu.make_async_copy(sparse_ref.at[b], blocks.at[b], block_sem.at[b])
        for b in range(n_blocks)
    ]
    ext_fetch = pltpu.make_async_copy(sent_ref.at[col], ext.at[col], local_sem.at[1])
    for fetch in fetches:
        fetch.start()
    ext_fetch.start()

    @pl.when(row == 0)
    def _():
        before[...] = jnp.zeros_like(before)
        up[...] = jnp.zeros_like(up)

    @pl.when(row == n_row - 1)
    def _():
        after[...] = jnp.zeros_like(after)
        down[...] = jnp.zeros_like(down)

    def to_row(source, target, index, step):
        return pltpu.make_async_remote_copy(
            src_ref=source,
            dst_ref=target,
            send_sem=row_send.at[index],
            recv_sem=row_recv.at[index],
            device_id=(row + step, col),
            device_id_type=MESH,
        )

    rising = [to_row(probe_ref, before, 0, 1), to_row(below, up, 1, 1)]
    falling = [to_row(probe_ref, after, 2, -1), to_row(above, down, 3, -1)]

    none = n_blocks * SLOTS
    for q in range(3):
        sums[q, none] = jnp.zeros((S, BLK), F32)
    def adjoint_regions(regions, begin, end):
        def step(b, carry):
            probe = adjoint_ref[:, pl.ds(pl.multiple_of(b * BLK, BLK), BLK)]
            for s in range(0, SLOTS, 2):
                for q in regions:
                    slot = q * SLOTS + s
                    pair = jnp.concatenate([blocks[b, slot], blocks[b, slot + 1]], axis=1)
                    product = jnp.dot(probe, pair, preferred_element_type=F32)
                    for i in range(2):
                        sums[q, b * SLOTS + s + i] = (
                            product[:, i * BLK : (i + 1) * BLK]
                            + sums[q, prior_ref[b, slot + i]]
                        )
            return carry

        lax.fori_loop(begin, end, step, 0)

    early = n_blocks // 2
    for fetch in fetches[:early]:
        fetch.wait()
    adjoint_regions((0, 2), 0, early)
    pl.semaphore_wait(barrier, n_col + 1)

    @pl.when(inner_up)
    def _():
        rising[0].start()

    @pl.when(inner_down)
    def _():
        falling[0].start()

    spread = [
        pltpu.make_async_remote_copy(
            src_ref=sent_ref.at[peer, k],
            dst_ref=ext.at[col, k],
            send_sem=ext_send.at[k, i],
            recv_sem=ext_recv.at[k, i],
            device_id=(row, peer),
            device_id_type=MESH,
        )
        for k in range(2)
        for i, peer in enumerate(peers)
    ]
    for copy in spread:
        copy.start()

    def product(b, regions):
        left = []
        right = []
        for q, source in regions:
            for s in range(q * SLOTS, (q + 1) * SLOTS):
                left.append(source[pattern_ref[row, b, s]])
                right.append(blocks[b, s])
        return lax.dot_general(
            jnp.concatenate(left, axis=1),
            jnp.concatenate(right, axis=1),
            (((1,), (1,)), ((), ())),
            preferred_element_type=F32,
        )

    for fetch in fetches[early:]:
        fetch.wait()
    adjoint_regions((0, 2), early, n_blocks)

    def settle(c, carry):
        above[c] = sums[0, final_ref[0, c]].astype(BF16)
        below[c] = sums[2, final_ref[2, c]].astype(BF16)
        return carry

    lax.fori_loop(0, n_blocks, settle, 0)

    @pl.when(inner_up)
    def _():
        rising[1].start()

    @pl.when(inner_down)
    def _():
        falling[1].start()

    def own_region(b, carry):
        lanes = pl.ds(pl.multiple_of(b * BLK, BLK), BLK)
        samples[0, :, lanes] = product(b, [(1, probe_ref)])
        return carry

    lax.fori_loop(0, n_blocks, own_region, 0)

    @pl.when(inner_down)
    def _():
        rising[0].wait_recv()

    @pl.when(inner_up)
    def _():
        falling[0].wait_recv()

    def other_regions(b, carry):
        lanes = pl.ds(pl.multiple_of(b * BLK, BLK), BLK)
        samples[0, :, lanes] += product(b, [(0, before), (2, after)])
        return carry

    lax.fori_loop(0, n_blocks, other_regions, 0)

    gram[...] = jnp.zeros_like(gram)
    row_id = lax.broadcasted_iota(jnp.int32, (BLK, BLK), 0)
    col_id = lax.broadcasted_iota(jnp.int32, (BLK, BLK), 1)
    quad = []

    def finish(k, other_terms):
        def assemble(h, carry):
            lanes = pl.ds(pl.multiple_of(h * 2 * BLK, 2 * BLK), 2 * BLK)
            y = ext[:, k, :, lanes].reshape(S, 2 * BLK).astype(F32) + other_terms(h, lanes)
            samples[k, :, lanes] = y
            gram[k] += dot3(y, y, ((1,), (1,)))
            return carry

        lax.fori_loop(0, n_blocks // 2, assemble, 0)
        last = gram[k, BLK:, BLK:]
        diagonal = jnp.sum(jnp.where(row_id == col_id, last, 0.0), axis=0, keepdims=True)
        pieces = (
            (0, gram[k, :BLK, BLK:]),
            (BLK, jnp.where(col_id >= row_id, gram[k, :BLK, :BLK], last)),
            (2 * BLK, jnp.broadcast_to(diagonal, (16, BLK))),
        )
        for at, piece in pieces:
            gram_ref[0, k, at : at + piece.shape[0]] = piece
            packed[k, at : at + piece.shape[0]] = piece.astype(BF16)
        copies = [
            pltpu.make_async_remote_copy(
                src_ref=packed.at[k],
                dst_ref=partner.at[i, k],
                send_sem=quad_send.at[3 * k + i],
                recv_sem=quad_recv.at[3 * k + i],
                device_id=(row, cx * side + other),
                device_id_type=MESH,
            )
            for i, other in enumerate((cy + 1 - 2 * (cy % 2), (cy + 2) % side, side - 1 - cy))
        ]
        for copy in copies:
            copy.start()
        quad.append(copies)

    ext_fetch.wait()
    for copy in spread[: n_col - 1]:
        copy.wait_recv()
    finish(0, lambda h, lanes: samples[0, :, lanes])
    adjoint_regions((1,), 0, n_blocks)
    for copy in spread[n_col - 1 :]:
        copy.wait_recv()

    @pl.when(inner_down)
    def _():
        rising[1].wait_recv()

    @pl.when(inner_up)
    def _():
        falling[1].wait_recv()

    def adjoint_terms(h, lanes):
        parts = []
        for c in range(2):
            at = h * 2 + c
            parts.append(sums[1, final_ref[1, at]] + down[at].astype(F32) + up[at].astype(F32))
        return jnp.concatenate(parts, axis=1)

    finish(1, adjoint_terms)
    store = pltpu.make_async_copy(samples, samples_ref, local_sem.at[2])
    store.start()

    @pl.when(inner_up)
    def _():
        for copy in rising:
            copy.wait_send()

    @pl.when(inner_down)
    def _():
        for copy in falling:
            copy.wait_send()

    for copy in spread:
        copy.wait_send()
    for k in range(2):
        quad[k][0].wait_recv()
        gram_ref[1, k] = gram_ref[0, k] + partner[0, k].astype(F32)
        quad[k][1].wait_recv()
        quad[k][2].wait_recv()
        gram_ref[2, k] = gram_ref[1, k] + partner[1, k].astype(F32) + partner[2, k].astype(F32)
    for copies in quad:
        for copy in copies:
            copy.wait_send()
    store.wait()


def exchange(pattern, prior, final, probe, adjoint_probe, sent, sparse):
    rows = sent.shape[3]
    leaves = sent.shape[0]
    held = 2 * BLK + 16
    anywhere = pl.BlockSpec(memory_space=pl.ANY)
    vmem = pl.BlockSpec(memory_space=pltpu.VMEM)
    dma = pltpu.SemaphoreType.DMA
    return pl.pallas_call(
        exchange_kernel,
        out_shape=[
            jax.ShapeDtypeStruct((2, S, rows), F32),
            jax.ShapeDtypeStruct((3, 2, held, BLK), F32),
        ],
        in_specs=[pl.BlockSpec(memory_space=pltpu.SMEM)] * 3 + [vmem] * 2 + [anywhere] * 2,
        out_specs=[anywhere, vmem],
        scratch_shapes=[
            pltpu.VMEM(sent.shape, BF16),
            pltpu.VMEM(probe.shape, BF16),
            pltpu.VMEM(probe.shape, BF16),
            pltpu.VMEM(probe.shape, BF16),
            pltpu.VMEM(probe.shape, BF16),
            pltpu.VMEM(probe.shape, BF16),
            pltpu.VMEM(probe.shape, BF16),
            pltpu.VMEM((3, sparse.shape[0] * SLOTS + 1, S, BLK), F32),
            pltpu.VMEM(sparse.shape, BF16),
            pltpu.VMEM((2, S, rows), F32),
            pltpu.VMEM((2, S, S), F32),
            pltpu.VMEM((2, held, BLK), BF16),
            pltpu.VMEM((3, 2, held, BLK), BF16),
            dma((2, leaves - 1)),
            dma((2, leaves - 1)),
            dma((4,)),
            dma((4,)),
            dma((6,)),
            dma((6,)),
            dma((3,)),
            dma((sparse.shape[0],)),
        ],
        compiler_params=pltpu.CompilerParams(
            collective_id=0, has_side_effects=True, vmem_limit_bytes=VMEM_LIMIT
        ),
        name="exchange",
    )(pattern, prior, final, probe, adjoint_probe, sent, sparse)


def splat(x, at):
    return jnp.broadcast_to(x[:, at:at+1], (8, BLK))

def eliminate(rows, first, half, lane, others):
    count=len(rows)
    for g in range(0, count, SUB):
        base=first+g
        e=[[splat(rows[g+j][half], base+i) if i>=j else None for i in range(SUB)] for j in range(SUB)]
        scale=[]; fac=[]
        for j in range(SUB):
            s=lax.rsqrt(e[j][j]); scale.append(s)
            f=[e[j][i]*s if i>j else None for i in range(SUB)]
            fac.append(f)
            for i in range(j+1,SUB):
                for l in range(i,SUB):
                    e[i][l]=e[i][l]-f[i]*f[l]
        share=-(-len(others)*SUB//(count-g))
        for other in others[:share]:
            other()
        others=others[share:]
        clean=[]
        for j in range(SUB):
            here=lane==base+j
            z=[x*scale[j] for x in rows[g+j]]
            z[half]=jnp.where(here,scale[j],z[half])
            rows[g+j]=z
            for i in range(j+1,SUB):
                r=list(rows[g+i]); r[half]=jnp.where(here,0.0,r[half])
                rows[g+i]=[x-fac[j][i]*y for x,y in zip(r,z)]
            c=list(z); c[half]=jnp.where((lane>base+j)&(lane<base+SUB),0.0,z[half]); clean.append(c)
        for i in range(g+SUB,count):
            r=list(rows[i]); r[half]=jnp.where((lane>=base)&(lane<base+SUB),0.0,r[half])
            for j in range(SUB):
                z=clean[j]
                f=splat(z[half], first+i)
                r=[x-f*y for x,y in zip(r,z)]
            rows[i]=r
    return rows

def factorize(work, count):
    lane = lax.broadcasted_iota(jnp.int32, (8, BLK), 1)
    others = []
    for lo in range(0, S, PANEL):
        half = lo // BLK
        rows = [
            [work[b][pl.ds(lo + i, 8, stride=PITCH), :] for b in range(2)] for i in range(PANEL)
        ]
        rows = eliminate(rows, lo - half * BLK, half, lane, others)
        for i in range(PANEL):
            for b in range(2):
                work[b][pl.ds(lo + i, 8, stride=PITCH), :] = rows[i][b]
        end = lo + PANEL
        if end == S:
            break
        skip = end // BLK
        row_id = lax.broadcasted_iota(jnp.int32, (PANEL, BLK), 0) + lo
        col_id = lax.broadcasted_iota(jnp.int32, (PANEL, BLK), 1) + BLK * half
        dead = (col_id > row_id) & (col_id < end)
        operands = []
        for m in range(count):
            base = m * PITCH
            panel = [work[b][base + lo : base + end, :] for b in range(2)]
            masked = [jnp.where(dead, 0.0, x) if b == half else x for b, x in enumerate(panel)]
            left = panel[1] if skip else jnp.concatenate(panel, axis=1)
            lh, lm, ll = split3(left)
            rh, rm, rl = split3(jnp.concatenate(masked, axis=1))
            operands.append(
                (
                    jnp.concatenate([lh, lh, lm, lh, ll, lm], axis=0).T,
                    jnp.concatenate([rh, rm, rh, rl, rh, rm], axis=0),
                )
            )

        def update(m, begin, stop, lo=lo, end=end, half=half, skip=skip, operands=operands):
            left, right = operands[m]
            product = jnp.dot(
                left[begin - skip * BLK : stop - skip * BLK], right, preferred_element_type=F32
            )
            cols = lax.broadcasted_iota(jnp.int32, (stop - begin, BLK), 1) + BLK * half
            mine = (cols >= lo) & (cols < end)
            base = m * PITCH
            for b in range(2):
                old = work[b][base + begin : base + stop, :]
                if b == half:
                    old = jnp.where(mine, 0.0, old)
                work[b][base + begin : base + stop, :] = old - product[:, b * BLK : (b + 1) * BLK]

        near = end + PANEL
        for m in range(count):
            update(m, end, near)
        others = []
        if near < S:
            others = [partial(update, m, near, S) for m in range(count)]


def load_grams(gram_ref, work):
    w0, w1 = work
    corner_row = lax.broadcasted_iota(jnp.int32, (BLK, BLK), 0)
    corner_col = lax.broadcasted_iota(jnp.int32, (BLK, BLK), 1)
    for m in range(8):
        held = gram_ref.at[m // 2 % 3, m % 2]
        shared = held[BLK : 2 * BLK]
        at = m * PITCH
        w0[at : at + BLK, :] = shared
        w1[at : at + BLK, :] = held[:BLK]
        w1[at + BLK : at + S, :] = jnp.where(
            corner_row == corner_col,
            jnp.broadcast_to(held[2 * BLK : 2 * BLK + 1], (BLK, BLK)),
            shared.T,
        )
        w0[at + BLK : at + S, :] = jnp.zeros((BLK, BLK), F32)


def factor_kernel(gram_ref, samples_ref, row_ref, col_ref, transfer_ref, w0, w1):
    work = (w0, w1)
    load_grams(gram_ref, work)
    factorize(work, 6)
    row_id = lax.broadcasted_iota(jnp.int32, (S, S), 0)
    col_id = lax.broadcasted_iota(jnp.int32, (S, S), 1)
    gain = math.sqrt(samples_ref.shape[2])
    for k in range(2):
        found = []
        for level in range(3):
            at = (2 * level + k) * PITCH
            found.append(jnp.concatenate([work[b][at : at + S, :] for b in range(2)], axis=1))
        inverse = [jnp.where(col_id <= row_id, x, 0.0) for x in found]
        upper = [
            jnp.where(col_id > row_id, x, jnp.where(col_id == row_id, 1.0 / x, 0.0))
            for x in found[:2]
        ]
        basis = dot3(inverse[0], samples_ref[k], ((1,), (0,))) * gain
        (row_ref, col_ref)[k][...] = basis.astype(BF16)
        for level in range(2):
            transfer_ref[k, level] = dot3(upper[level], inverse[level + 1], ((1,), (1,)))


def factor(grams, samples):
    rows = samples.shape[2]
    vmem = pl.BlockSpec(memory_space=pltpu.VMEM)
    return pl.pallas_call(
        factor_kernel,
        out_shape=[
            jax.ShapeDtypeStruct((S, rows), BF16),
            jax.ShapeDtypeStruct((S, rows), BF16),
            jax.ShapeDtypeStruct((2, 2, S, S), F32),
        ],
        in_specs=[vmem] * 2,
        out_specs=[vmem] * 3,
        scratch_shapes=[pltpu.VMEM((8 * PITCH, BLK), F32)] * 2,
        compiler_params=params(),
        name="factor",
    )(grams, samples)


def local(
    child_samples, child_map, forward_probe, adjoint_probe, stored_sparse_blocks, block_pattern
):
    leaves = lax.axis_size("col")
    sent, blocked, prior, final = extend(
        child_map, block_pattern, child_samples, forward_probe, leaves
    )
    samples, grams = exchange(
        block_pattern, prior, final, blocked, adjoint_probe, sent, stored_sparse_blocks
    )
    return tuple(factor(grams, samples))


def solution(mesh):
    return jax.shard_map(
        local,
        mesh=mesh,
        in_specs=(
            P(None, None, "col", "row"),
            P(None, "row"),
            P(None, ("row", "col")),
            P(None, ("row", "col")),
            P(("row", "col"), None, None, None),
            P(None, "col", None),
        ),
        out_specs=(
            P(None, ("row", "col")),
            P(None, ("row", "col")),
            P(None, None, ("row", "col"), None),
        ),
        check_vma=False,
    )
```
